32 devices in a mesh: expert: 16 (over z, x, core), tensor: 2 (over y).
Axes of the slice: x: 2, y: 2, z: 4, core: 2. Of those that a mesh axis runs over, the one named last changes fastest.
Arguments:
- query: bfloat16 [128, 8192], P(('expert', 'tensor')), may hold values from -6 to 6
- cache_keys: bfloat16 [128, 128, 4, 128], P(('expert', 'tensor')), may hold values from -6 to 6
- cache_values: bfloat16 [128, 128, 4, 128], P(('expert', 'tensor')), may hold values from -6 to 6
- lengths: int32 [128], P(('expert', 'tensor')), may hold values from 2 to 128, as said below
- residual: bfloat16 [128, 4096], P('tensor', 'expert'), may hold values from -12 to 12
- out_proj: bfloat16 [4096, 8192], P('expert', 'tensor'), may hold values from -0.0625 to 0.0625
- norm_gain: bfloat16 [4096], P('expert'), may hold values from 0.099609375 to 1.8984375
- expert_ids: int32 [128, 8], replicated, may hold values from 0 to 15, all different within a row; in each aligned block of 128 rows (0 to 127, 128 to 255, ...) at most 128 rows name the same one
- gate_scores: bfloat16 [128, 8], replicated, may hold values from 0.019897461 to 1
- w_gate: bfloat16 [16, 1536, 4096], P('expert', 'tensor'), may hold values from -0.09375 to 0.09375
- w_up: bfloat16 [16, 1536, 4096], P('expert', 'tensor'), may hold values from -0.09375 to 0.09375
- w_down: bfloat16 [16, 1536, 4096], P('expert', 'tensor'), may hold values from -0.15625 to 0.15625
Outputs:
- attn_residual: bfloat16 [128, 4096], P('tensor', 'expert')
- expert_mix: bfloat16 [128, 4096], P('tensor', 'expert')
The draws below stay inside these ranges and needn't reach their ends.
Inputs may be any that keep to these rules, and one draw needn't show every extreme that they name: `expert_ids`: each row names 8 different experts; no expert is named by more than 128 rows, and one by exactly 128. `lengths`: some row has exactly 128.
All inputs are finite; a program needn't handle non-finite values.
Results may differ from the reference program's by a relative error of at most 0.018.
Values may be sent and summed in bfloat16 or wider, within the bound.
A program may use at most 64 MiB of HBM per device.

```python
import math
import jax
import jax.numpy as jnp
import numpy as np
from jax import lax

D = 4096
HEADS = 64
KV_HEADS = 4
HEAD_DIM = 128
FF = 1536
TOPK = 8
CACHE = 128
ROWS = 128
EXPERTS = 16
CAP = 128


def draw_query(key, part):
    blended = jnp.clip(jax.random.normal(jax.random.fold_in(key, 11), (ROWS, HEADS, HEAD_DIM), jnp.float32), -6.0, 6.0)
    return blended.reshape(ROWS, HEADS * HEAD_DIM).astype(jnp.bfloat16)


def draw_cache_keys(key, part):
    key_shape = (ROWS, CACHE, KV_HEADS, HEAD_DIM)
    drawn_draw = jnp.clip(jax.random.normal(jax.random.fold_in(key, 12), key_shape, jnp.float32), -6.0, 6.0)
    return drawn_draw.astype(jnp.bfloat16)


def draw_lengths(key, part):
    drawn = jax.random.randint(jax.random.fold_in(key, 21), (ROWS,), 2, CACHE + 1, dtype=jnp.int32)
    marked = jax.random.randint(jax.random.fold_in(key, 22), (), 0, ROWS, dtype=jnp.int32)
    return jnp.where(jnp.arange(ROWS, dtype=jnp.int32) == marked, CACHE, drawn).astype(jnp.int32)


def draw_residual(key, part):
    rising = 3.0 ** (jnp.arange(D, dtype=jnp.float32) / D)
    column_scale = jnp.exp(jax.random.uniform(jax.random.fold_in(key, 31), (D,), jnp.float32, 0.0, math.log(3.0)))
    base_draw = jnp.clip(jax.random.normal(jax.random.fold_in(key, 32), (ROWS, D), jnp.float32), -5.0, 5.0)
    row_scale = jnp.exp(jax.random.uniform(jax.random.fold_in(key, 34), (ROWS, 1), jnp.float32, math.log(0.3), math.log(3.0)))
    drawn = base_draw * rising[None, :] * column_scale[None, :] * row_scale * 0.3
    return jnp.clip(drawn, -12.0, 12.0).astype(jnp.bfloat16)


def steps_of(key, extent, cuts, least, high):
    gain = 1.0
    for position, blocks in cuts:
        draws = jax.random.uniform(jax.random.fold_in(jax.random.fold_in(key, 6), position), (blocks,), jnp.float32, least / len(cuts), high / len(cuts))
        gain = gain * jnp.repeat(jnp.exp(draws), extent[position] // blocks).reshape((-1,) + (1,) * (len(extent) - 1 - position))
    return gain


def assign_block(stream_key, own, number, rows, amount, top, bound, skew):
    order = jax.random.permutation(stream_key, amount)
    heavy_load, usual = load_shares(amount, rows * top, bound, skew, True), load_shares(amount, rows * top, bound, skew, False)
    places = jnp.arange(amount)

    def named(sizes, rotation):
        used = int((sizes > 0).sum())
        fixed = max(1, used // 4)
        passed = fixed + (places - fixed + rotation * (used - fixed)) % max(1, amount - fixed)
        return jnp.zeros((amount,), jnp.int32).at[order[jnp.where(places < fixed, places, passed)]].set(jnp.asarray(sizes, jnp.int32))

    sizes = jnp.where(number % 4 == 0, named(heavy_load, number // 4), named(usual, number - number // 4 - 1))
    mixed = jax.random.permutation(jax.random.fold_in(own, 3), amount)
    giver, sink = mixed[0:amount // 2 * 2:2], mixed[1:amount // 2 * 2:2]
    margin = jnp.minimum(sizes[giver] - 1, bound - sizes[sink]) // 2
    margin = jnp.where((giver == order[0]) | (sink == order[0]) | (sizes[sink] == 0), 0, jnp.maximum(margin, 0))
    passed = jax.random.randint(jax.random.fold_in(own, 4), (amount // 2,), 0, 1 << 20) % (margin + 1)
    sizes = sizes.at[giver].add(-passed).at[sink].add(passed)
    members = jnp.searchsorted(jnp.cumsum(sizes), jnp.arange(rows * top), side="right").astype(jnp.int32)
    listing = members.reshape(top, rows).T
    listing = listing[jax.random.permutation(jax.random.fold_in(own, 1), rows)]
    rotation = jax.random.randint(jax.random.fold_in(own, 2), (rows, 1), 0, top)
    return jnp.take_along_axis(listing, (jnp.arange(top)[None, :] + rotation) % top, axis=1)


def load_shares(number_of, total, reach, slope, full):
    loads = [(1 << 20) // math.isqrt(standing ** slope) + 1 for standing in range(1, number_of + 1)]
    largest = reach if full else min(reach, max(-(-total // number_of), total * loads[0] // sum(loads)))
    least = 1 if total - largest >= number_of - 1 else 0
    counts, rest = [largest] + [least] * (number_of - 1), total - largest - least * (number_of - 1)
    while rest > 0:
        free = [i for i in range(1, number_of) if counts[i] < largest] or [i for i in range(1, number_of) if counts[i] < reach]
        pool, remaining = sum([loads[i] for i in free]), rest
        for i in free:
            extra = min(reach - counts[i], max(1, remaining * loads[i] // pool), rest)
            counts[i] = counts[i] + extra
            rest = rest - extra
    return np.array(counts)


def scatter_about(key, dims, deviation, most, shards=(), kind=jnp.bfloat16):
    values = jax.random.normal(key, dims, jnp.float32) * deviation
    if len(shards) > 0:
        values = steps_of(key, dims, shards, -0.22, 0.18) * values
    return jnp.clip(values, min=-most, max=most).astype(kind)


def setup_inputs(seed: int = 0) -> dict:
    arg_keys = jax.random.split(jax.random.key(seed), 13)
    query = draw_query(jax.random.fold_in(arg_keys[12], 71), 0)
    cache_keys = draw_cache_keys(jax.random.fold_in(arg_keys[12], 71), 0)
    cache_values = scatter_about(arg_keys[2], (ROWS, CACHE, KV_HEADS, HEAD_DIM), 1.0, 6.0, ((0, 32),))
    lengths = draw_lengths(jax.random.fold_in(arg_keys[12], 71), 0)
    residual = draw_residual(jax.random.fold_in(arg_keys[12], 71), 0)
    out_proj = scatter_about(arg_keys[5], (D, HEADS * HEAD_DIM), (HEADS * HEAD_DIM) ** -0.5, 0.0625, ((0, 16), (1, 2)))
    norm_gain = jnp.clip(1.0 + 0.18 * jax.random.normal(arg_keys[6], (D,), jnp.float32), 0.099609375, 1.8984375).astype(jnp.bfloat16)
    expert_ids_keys = jax.random.split(jax.random.fold_in(arg_keys[7], 1), ROWS // ROWS)
    expert_ids_turns = jax.random.permutation(jax.random.fold_in(arg_keys[7], 3), ROWS // ROWS)
    expert_ids = jax.vmap(lambda own, number: assign_block(jax.random.fold_in(arg_keys[7], 2), own, number, ROWS, EXPERTS, TOPK, CAP, 2))(expert_ids_keys, expert_ids_turns).reshape((ROWS, TOPK))
    gate_scores = jnp.clip(jnp.exp(jax.random.uniform(arg_keys[8], (ROWS, TOPK), jnp.float32, math.log(0.019897461), math.log(1.0))), 0.019897461, 1.0).astype(jnp.bfloat16)
    w_gate = scatter_about(arg_keys[9], (EXPERTS, FF, D), D ** -0.5, 0.09375, ((0, 16), (1, 2)))
    w_up = scatter_about(arg_keys[10], (EXPERTS, FF, D), D ** -0.5, 0.09375, ((0, 16), (1, 2)))
    w_down = scatter_about(arg_keys[11], (EXPERTS, FF, D), FF ** -0.5, 0.15625, ((0, 16), (1, 2)))
    return dict(query=query, cache_keys=cache_keys, cache_values=cache_values, lengths=lengths, residual=residual, out_proj=out_proj, norm_gain=norm_gain, expert_ids=expert_ids, gate_scores=gate_scores, w_gate=w_gate, w_up=w_up, w_down=w_down)


def reference(query, cache_keys, cache_values, lengths, residual, out_proj, norm_gain, expert_ids, gate_scores, w_gate, w_up, w_down):
    group_size = HEADS // KV_HEADS
    grouped = query.astype(jnp.float32).reshape(ROWS, KV_HEADS, group_size, HEAD_DIM)
    scores = jnp.einsum('rkgd,rpkd->rkgp', grouped, cache_keys.astype(jnp.float32)) * HEAD_DIM ** (-0.5)
    usable = jnp.arange(CACHE, dtype=jnp.int32)[None, :] < lengths[:, None]
    usable_mask = usable[:, None, None, :]
    peak = lax.optimization_barrier(jnp.max(jnp.where(usable_mask, scores, -jnp.inf), axis=-1, keepdims=True))
    raw_weights = jnp.where(usable_mask, jnp.exp(scores - peak), 0.0)
    attn_weights = raw_weights / lax.optimization_barrier(jnp.sum(raw_weights, axis=-1, keepdims=True))
    context = jnp.einsum('rkgp,rpkd->rkgd', attn_weights, cache_values.astype(jnp.float32))
    context = context.reshape(ROWS, HEADS * HEAD_DIM).astype(jnp.bfloat16)
    attn_out = jnp.dot(context, out_proj.T, preferred_element_type=jnp.float32)
    hidden_state = residual.astype(jnp.float32) + attn_out
    mean_square = lax.optimization_barrier(jnp.mean(hidden_state * hidden_state, axis=1, keepdims=True))
    normed = (hidden_state * lax.rsqrt(mean_square + 1e-06) * norm_gain.astype(jnp.float32)[None, :]).astype(jnp.bfloat16)
    gate_weight = gate_scores.astype(jnp.float32)
    gate_weight = gate_weight / lax.optimization_barrier(jnp.sum(gate_weight, axis=1, keepdims=True))
    flat_ids = expert_ids.reshape(-1).astype(jnp.int32)
    onehot = (flat_ids[:, None] == jnp.arange(EXPERTS, dtype=jnp.int32)[None, :]).astype(jnp.int32)
    slot_index = lax.optimization_barrier(jnp.sum((jnp.cumsum(onehot, axis=0) - onehot) * onehot, axis=1)).astype(jnp.int32)
    destination = (flat_ids * CAP + slot_index).astype(jnp.int32)
    source = (jnp.arange(ROWS * TOPK, dtype=jnp.int32) // TOPK).astype(jnp.int32)
    slot_owner = jnp.full((EXPERTS * CAP,), -1, jnp.int32).at[destination].set(source).reshape(EXPERTS, CAP)

    def expert_block(pieces):
        owners, gate_mat, up_mat, down_mat = pieces
        rows_in = jnp.where((owners >= 0)[:, None], normed[jnp.maximum(owners, 0)], jnp.zeros((), jnp.bfloat16))
        gate_proj = jnp.dot(rows_in, gate_mat.T, preferred_element_type=jnp.float32)
        up_proj = jnp.dot(rows_in, up_mat.T, preferred_element_type=jnp.float32)
        activation = (jax.nn.silu(gate_proj) * up_proj).astype(jnp.bfloat16)
        return jnp.dot(activation, down_mat, preferred_element_type=jnp.float32)
    expert_result = lax.map(expert_block, (slot_owner, w_gate, w_up, w_down))
    picked = expert_result.reshape(EXPERTS * CAP, D)[destination].reshape(ROWS, TOPK, D)
    expert_mix = lax.optimization_barrier(jnp.sum(picked * gate_weight[:, :, None], axis=1)).astype(jnp.bfloat16)
    return (hidden_state.astype(jnp.bfloat16), expert_mix)
```

```python
import jax
import jax.numpy as jnp
from jax import lax
from jax.experimental import pallas as pl
from jax.experimental.pallas import tpu as pltpu
from jax.sharding import PartitionSpec as P

floor_value = -1e30
epsilon = 1e-06


def softmax_parts(queries, key_block, value_block, usable, score_scale):
    scores = (
        jnp.einsum("rkgd,rpkd->rkgp", queries, key_block, preferred_element_type=jnp.float32)
        * score_scale
    )
    usable_mask = usable[:, None, None, :]
    peak = jnp.max(jnp.where(usable_mask, scores, floor_value), axis=-1)
    raw_weights = jnp.where(usable_mask, jnp.exp(scores - peak[..., None]), 0.0)
    weight_sum = jnp.sum(raw_weights, axis=-1)
    weighted = jnp.einsum("rkgp,rpkd->rkgd", raw_weights, value_block.astype(jnp.float32))
    return (weight_sum, weighted)


def body(
    query,
    cache_keys,
    cache_values,
    lengths,
    residual,
    out_proj,
    norm_gain,
    expert_ids,
    gate_scores,
    w_gate,
    w_up,
    w_down,
):
    row_count, full_heads_width = query.shape
    cache_len = cache_keys.shape[1]
    kv_count = cache_keys.shape[2]
    head_size = cache_keys.shape[3]
    head_count = full_heads_width // head_size
    group_size = head_count // kv_count
    score_scale = head_size ** (-0.5)
    usable = jnp.arange(cache_len, dtype=jnp.int32)[None, :] < lengths[:, None]
    grouped = query.reshape(row_count, kv_count, group_size, head_size)
    weight_sum, weighted = softmax_parts(grouped, cache_keys, cache_values, usable, score_scale)
    context_rows_own = (
        (weighted / weight_sum[..., None]).astype(jnp.bfloat16).reshape(row_count, full_heads_width)
    )
    context = lax.all_to_all(context_rows_own, "tensor", split_axis=1, concat_axis=0, tiled=True)
    attn_part = jnp.dot(
        lax.all_gather(context, "expert", axis=0, tiled=True),
        out_proj.T,
        preferred_element_type=jnp.float32,
    )
    attn_share = lax.psum_scatter(attn_part, "tensor", scatter_dimension=0, tiled=True)
    hidden_state = residual.astype(jnp.float32) + attn_share
    squares = lax.psum(jnp.sum(hidden_state * hidden_state, axis=1), "expert")
    full_width = hidden_state.shape[1] * lax.axis_size("expert")
    scaled_share = (hidden_state * norm_gain.astype(jnp.float32)[None, :]).astype(jnp.bfloat16)
    scaled = lax.all_gather(
        lax.all_gather(scaled_share, "tensor", axis=0, tiled=True), "expert", axis=1, tiled=True
    )
    mean_all = lax.all_gather(squares / full_width, "tensor", axis=0, tiled=True)
    row_scale = lax.rsqrt(mean_all + epsilon)[:, None]
    experts_local = w_gate.shape[0]
    gate_weight = gate_scores.astype(jnp.float32)
    gate_weight = gate_weight / jnp.sum(gate_weight, axis=1, keepdims=True)
    mixed = None
    for local in range(experts_local):
        expert = lax.axis_index("expert") * experts_local + local
        weight = jnp.sum(jnp.where(expert_ids == expert, gate_weight, 0.0), axis=1, keepdims=True)
        gate_proj = row_scale * lax.dot_general(
            scaled, w_gate[local], (((1,), (1,)), ((), ())), preferred_element_type=jnp.float32
        )
        up_proj = row_scale * lax.dot_general(
            scaled, w_up[local], (((1,), (1,)), ((), ())), preferred_element_type=jnp.float32
        )
        activation = (jax.nn.silu(gate_proj) * up_proj).astype(jnp.bfloat16)
        part = weight * jnp.dot(activation, w_down[local], preferred_element_type=jnp.float32)
        mixed = part if mixed is None else mixed + part
    mixed = lax.psum_scatter(
        mixed.astype(jnp.bfloat16), "tensor", scatter_dimension=0, tiled=True
    )
    mixed_share = lax.psum_scatter(mixed, "expert", scatter_dimension=1, tiled=True)
    return (hidden_state.astype(jnp.bfloat16), mixed_share)


MESH = pl.DeviceIdType.MESH
NZ = 4
ACROSS, CORE = 4, 8


def remote(src, dst, send, recv, device):
    return pltpu.make_async_remote_copy(
        src_ref=src, dst_ref=dst, send_sem=send, recv_sem=recv, device_id=device, device_id_type=MESH
    )


class Gather:
    def __init__(self, buf, sends, recvs, place, order):
        self.buf, self.sends, self.recvs = buf, sends, recvs
        self.z, self.x, self.c, self.y = place
        self.order = order

    def slot(self, zz, xx, cc):
        return zz * 4 + xx * 2 + cc

    def copy(self, slot, send, recv, target):
        return remote(
            self.buf.at[slot], self.buf.at[slot], self.sends.at[send], self.recvs.at[recv], (target, self.y)
        )

    def z_copy(self, zz):
        z, x, c = self.z, self.x, self.c
        return self.copy(self.slot(z, x, c), zz, z, self.slot(zz, x, c))

    def z_landing(self, zz):
        z, x, c = self.z, self.x, self.c
        return self.copy(self.slot(zz, x, c), z, zz, self.slot(zz, x, c))

    def x_copy(self, zz):
        z, x, c = self.z, self.x, self.c
        return self.copy(self.slot(zz, x, c), ACROSS + zz, ACROSS + zz, self.slot(z, 1 - x, c))

    def x_landing(self, zz):
        z, x, c = self.z, self.x, self.c
        return self.copy(self.slot(zz, 1 - x, c), ACROSS + zz, ACROSS + zz, self.slot(z, 1 - x, c))

    def core_copy(self, zz, xx, cc):
        sem = CORE + xx * NZ + zz
        return self.copy(self.slot(zz, xx, cc), sem, sem, self.slot(self.z, self.x, 1 - self.c))

    def begin(self):
        for i in range(NZ - 1):
            self.z_copy(self.order[i]).start()
        self.x_copy(self.z).start()
        self.core_copy(self.z, self.x, self.c).start()
        return self.slot(self.z, self.x, self.c)

    def take_z(self, i):
        zz = self.order[NZ - 1 - i]
        self.z_landing(zz).wait_recv()
        self.x_copy(zz).start()
        self.core_copy(zz, self.x, self.c).start()
        return self.slot(zz, self.x, self.c)

    def take_x(self, i):
        zz = self.order[NZ - 1 - i]
        self.x_landing(zz).wait_recv()
        self.core_copy(zz, 1 - self.x, self.c).start()
        return self.slot(zz, 1 - self.x, self.c)

    def take_core(self, i, near):
        zz = self.order[NZ - 1 - i]
        xx = self.x if near else 1 - self.x
        self.core_copy(zz, xx, 1 - self.c).wait_recv()
        return self.slot(zz, xx, 1 - self.c)

    def wait_sends(self):
        for i in range(NZ):
            zz = self.order[i]
            if i < NZ - 1:
                self.z_copy(zz).wait_send()
            self.x_copy(zz).wait_send()
            for xx in range(2):
                self.core_copy(zz, xx, self.c).wait_send()


def nt_dot(a, b):
    return lax.dot_general(a, b, (((1,), (1,)), ((), ())), preferred_element_type=jnp.float32)


def layer_kernel(
    q_ref, k_hbm, v_hbm, len_ref, res_ref, wo_hbm, gain_ref, ids_ref, gates_ref,
    wg_hbm, wu_hbm, wd_hbm,
    out_ref,
    k_v, v_v, wo_v, wg_v, wu_v, wd_v, local_sems,
    lay, qlay, sblk, ctx, res_all, part, part_out, part_in, hid_all,
    gate_acc, up_acc, act, mine, core_out, core_in, x_out, x_in, y_out, y_in, d_out, d_in, z_out, z_in,
    c_send, c_recv, h_send, h_recv, p_send, p_recv, r_send, r_recv,
):
    f32, bf16 = jnp.float32, jnp.bfloat16
    e = lax.axis_index("expert")
    y = lax.axis_index("tensor")
    z, x, c = e // 4, (e // 2) % 2, e % 2
    ex, ec = e + 2 * (1 - 2 * x), e + 1 - 2 * c
    mirror = z // 2
    near_z = z + mirror * (3 - 2 * z)
    order = [o + mirror * (3 - 2 * o) for o in (3, 2, 1 - near_z, near_z)]
    barrier = pltpu.get_barrier_semaphore()
    pairs = [(k_hbm, k_v), (v_hbm, v_v), (wo_hbm, wo_v), (wg_hbm, wg_v), (wu_hbm, wu_v), (wd_hbm, wd_v)]
    loads = [pltpu.make_async_copy(s, d, local_sems.at[i]) for i, (s, d) in enumerate(pairs)]
    loads[0].start()
    loads[1].start()
    peers = [(ec, y), (ex, y), (e, 1 - y), (ex, 1 - y)]
    peers += [(order[i] * 4 + x * 2 + c, y) for i in range(NZ - 1)]
    for dev in peers:
        pl.semaphore_signal(barrier, inc=1, device_id=dev, device_id_type=MESH)

    rows = q_ref.shape[0]
    for h in range(64):
        qlay[h * 8 : h * 8 + rows, :] = q_ref[:, h * 128 : (h + 1) * 128].astype(f32)
    res_all[y] = res_ref[...]
    loads[0].wait()
    loads[1].wait()
    for d in loads[2:]:
        d.start()
    col = lax.broadcasted_iota(jnp.int32, (64, 512), 1)
    head = lax.broadcasted_iota(jnp.int32, (64, 512), 0)
    same = (col % 4) == (head // 16)
    for r in range(rows):
        q = qlay[pl.ds(r, 64, stride=8), :].astype(bf16)
        s = nt_dot(q, k_v[r]) * (128 ** -0.5)
        ok = same & ((col // 4) < len_ref[r])
        peak = jnp.max(jnp.where(ok, s, -1e30), axis=1, keepdims=True)
        w = jnp.where(ok, jnp.exp(s - peak), 0.0)
        total = jnp.sum(w, axis=1, keepdims=True)
        o = jnp.dot(w.astype(bf16), v_v[r], preferred_element_type=f32) / total
        for half in range(2):
            for j in range(4):
                h0 = half * 32 + j * 8
                lay[pl.ds(half * 128 + 4 * j + r, 8, stride=16), :] = o[h0 : h0 + 8]
    for half in range(2):
        for hh in range(8):
            t = (half * 8 + hh) * 16
            sblk[half, :, hh * 128 : (hh + 1) * 128] = lay[t : t + 16, :].astype(bf16)
    ctx[e, y] = sblk[y]
    pl.semaphore_wait(barrier, 7)

    swap = remote(sblk.at[1 - y], ctx.at[e, y], p_send.at[0], p_recv.at[0], (e, 1 - y))
    swap.start()
    rsend = remote(res_all.at[y], res_all.at[y], p_send.at[2], p_recv.at[2], (e, 1 - y))
    rsend.start()
    swap.wait_recv()
    g1 = Gather(ctx, c_send, c_recv, (z, x, c, y), order)
    g1.begin()
    for i in range(1, NZ):
        g1.take_z(i)
        g1.take_x(i - 1)
    g1.take_x(NZ - 1)
    for i in range(NZ):
        g1.take_core(i, True)
        g1.take_core(i, False)

    loads[2].wait()
    lhs = ctx.reshape(512, 1024)
    quarter = (lax.broadcasted_iota(jnp.int32, (512, 256), 0) % 16) // 4
    acc = jnp.zeros((512, 256), f32)
    for j in range(4):
        pj = nt_dot(lhs[...], wo_v[:, j * 1024 : (j + 1) * 1024])
        acc = jnp.where(quarter == j, pj, acc)
    folded = acc.reshape(32, 2, 8, 256)
    folded = (folded[:, 0] + folded[:, 1]).reshape(256, 256)
    low = (lax.broadcasted_iota(jnp.int32, (256, 256), 0) % 8) < 4
    folded = folded + jnp.where(low, pltpu.roll(folded, 252, 0), pltpu.roll(folded, 4, 0))
    folded = folded.reshape(16, 2, 8, 256)
    low3 = lax.broadcasted_iota(jnp.int32, (16, 8, 256), 1) < 4
    part[...] = jnp.where(low3, folded[:, 0], folded[:, 1]).reshape(2, 64, 256)
    part_out[...] = part[...].astype(bf16)
    psend = remote(part_out, part_in, p_send.at[1], p_recv.at[1], (e, 1 - y))
    psend.start()
    rsend.wait_recv()
    psend.wait_recv()
    part[...] = res_all[...].astype(f32) + (part[...] + part_in[...].astype(f32))
    hidden = part[...].reshape(128, 256)
    hid_all[e, 0:128] = (hidden * gain_ref[...].astype(f32).reshape(1, 256)).astype(bf16)
    ss = jnp.sum(hidden * hidden, axis=1, keepdims=True)
    eye = lax.broadcasted_iota(jnp.int32, (128, 128), 0) == lax.broadcasted_iota(jnp.int32, (128, 128), 1)
    sq = jnp.sum(jnp.where(eye, ss, 0.0), axis=0, keepdims=True)
    sq_high = sq.astype(bf16).astype(f32)
    hid_all[e, 128:144, 0:128] = jnp.broadcast_to(sq_high, (16, 128)).astype(bf16)
    hid_all[e, 128:144, 128:256] = jnp.broadcast_to(sq - sq_high, (16, 128)).astype(bf16)
    g2 = Gather(hid_all, h_send, h_recv, (z, x, c, y), order)

    def products(slots, first=False):
        def step(n, _):
            rows_n = pl.ds(pl.multiple_of(n * 256, 256), 256)
            for wref, aref in ((wg_v, gate_acc), (wu_v, up_acc)):
                a = None if first else aref[n]
                for src in slots:
                    cols = pl.ds(pl.multiple_of(src * 256, 256), 256)
                    t = nt_dot(hid_all[src, 0:128], wref[rows_n, cols])
                    a = t if a is None else a + t
                aref[n] = a
            return 0

        lax.fori_loop(0, 3, step, 0)

    slot0 = g2.begin()
    out_ref[0] = part[y]
    loads[3].wait()
    loads[4].wait()
    products([slot0], True)
    for i in range(1, NZ):
        za = g2.take_z(i)
        xa = g2.take_x(i - 1)
        if i < NZ - 1:
            products([za, xa])
    products([za, xa] + [g2.take_core(i, near) for i in range(2) for near in (True, False)])
    xa = g2.take_x(NZ - 1)
    products([xa, g2.take_core(2, True), g2.take_core(2, False), g2.take_core(3, True)])
    products([g2.take_core(3, False)])

    tail = jnp.sum(hid_all[:, 128:144, :].astype(f32), axis=0)[0:1]
    scale_row = lax.rsqrt((tail[:, 0:128] + tail[:, 128:256]) / 4096.0 + epsilon)
    scale = jnp.sum(jnp.where(eye, scale_row, 0.0), axis=1, keepdims=True)
    gw = gates_ref[...].astype(f32)
    gw = gw / jnp.sum(gw, axis=0, keepdims=True)
    weight_row = jnp.sum(jnp.where(ids_ref[...] == e, gw, 0.0), axis=0, keepdims=True)
    weight = jnp.sum(jnp.where(eye, weight_row, 0.0), axis=1, keepdims=True)
    for n in range(3):
        g = gate_acc[n] * scale
        u = up_acc[n] * scale
        a = (g / (1.0 + jnp.exp(-g)) * u * weight).astype(bf16)
        for half in range(2):
            to = pl.ds(pl.multiple_of(((half + y) % 2) * 64, 64), 64)
            act[to, n * 256 : (n + 1) * 256] = a[half * 64 : (half + 1) * 64]
    loads[5].wait()

    def block(zz, xx, cc):
        cols = pl.ds(pl.multiple_of((zz * 4 + xx * 2 + cc) * 256, 256), 256)
        return jnp.dot(act[...], wd_v[:, cols], preferred_element_type=f32)

    def core_copy(zz, k):
        b = k * NZ + zz
        return remote(core_out.at[b], core_in.at[b], r_send.at[b], r_recv.at[b], (ec, y))

    def x_copy(zz):
        return remote(x_out.at[zz], x_in.at[zz], r_send.at[8 + zz], r_recv.at[8 + zz], (ex, y))

    def y_copy(zz):
        return remote(y_out.at[zz], y_in.at[zz], r_send.at[12 + zz], r_recv.at[12 + zz], (e, 1 - y))

    def d_copy(zz):
        return remote(d_out.at[zz], d_in.at[zz], r_send.at[16 + zz], r_recv.at[16 + zz], (ex, 1 - y))

    def z_copy(zz):
        return remote(
            z_out.at[zz], z_in.at[z], r_send.at[20 + zz], r_recv.at[20 + z], (zz * 4 + x * 2 + c, y)
        )

    def z_landing(zz):
        return remote(
            z_out.at[zz], z_in.at[zz], r_send.at[20 + z], r_recv.at[20 + zz], (zz * 4 + x * 2 + c, y)
        )

    def to_core(zz):
        for k, xx in enumerate((1 - x, x)):
            core_out[k * NZ + zz] = block(zz, xx, 1 - c).astype(bf16)
            core_copy(zz, k).start()

    def to_plane(zz):
        far = block(zz, 1 - x, c)
        core_copy(zz, 0).wait_recv()
        far = far + core_in[zz].astype(f32)
        d_out[zz] = far[64:128].astype(bf16)
        d_copy(zz).start()
        x_out[zz] = far[0:64].astype(bf16)
        x_copy(zz).start()
        near = block(zz, x, c)
        core_copy(zz, 1).wait_recv()
        near = near + core_in[NZ + zz].astype(f32)
        y_out[zz] = near[64:128].astype(bf16)
        y_copy(zz).start()
        mine[zz] = near[0:64]

    def plane_sum(zz):
        x_copy(zz).wait_recv()
        y_copy(zz).wait_recv()
        d_copy(zz).wait_recv()
        return mine[zz] + x_in[zz].astype(f32) + (y_in[zz].astype(f32) + d_in[zz].astype(f32))

    to_core(order[0])
    for i in range(NZ):
        if i < NZ - 1:
            to_core(order[i + 1])
        to_plane(order[i])
    for i in range(NZ - 1):
        zz = order[i]
        z_out[zz] = plane_sum(zz).astype(bf16)
        z_copy(zz).start()
    fin = plane_sum(z)
    for i in range(NZ - 2, -1, -1):
        zz = order[i]
        z_landing(zz).wait_recv()
        fin = fin + z_in[zz].astype(f32)
    out_ref[1] = fin

    for d in (swap, psend, rsend):
        d.wait_send()
    g1.wait_sends()
    g2.wait_sends()
    for i in range(NZ):
        zz = order[i]
        core_copy(zz, 0).wait_send()
        core_copy(zz, 1).wait_send()
        x_copy(zz).wait_send()
        y_copy(zz).wait_send()
        d_copy(zz).wait_send()
        if i < NZ - 1:
            z_copy(zz).wait_send()


def fused_body(
    query, cache_keys, cache_values, lengths, residual, out_proj, norm_gain, expert_ids, gate_scores,
    w_gate, w_up, w_down,
):
    f32, bf16 = jnp.float32, jnp.bfloat16
    rows = query.shape[0]
    keys = cache_keys.reshape(rows, 512, 128)
    values = cache_values.reshape(rows, 512, 128)
    vm = pl.BlockSpec(memory_space=pltpu.VMEM)
    hb = pl.BlockSpec(memory_space=pl.ANY)
    sm = pl.BlockSpec(memory_space=pltpu.SMEM)
    V, S = pltpu.VMEM, pltpu.SemaphoreType.DMA
    out = pl.pallas_call(
        layer_kernel,
        name="layer",
        out_shape=jax.ShapeDtypeStruct((2, 64, 256), f32),
        in_specs=[vm, hb, hb, sm, vm, hb, vm, vm, vm, hb, hb, hb],
        out_specs=vm,
        scratch_shapes=[
            V((rows, 512, 128), bf16), V((rows, 512, 128), bf16), V((256, 4096), bf16),
            V((768, 4096), bf16), V((768, 4096), bf16), V((768, 4096), bf16), S((6,)),
            V((256, 128), f32), V((512, 128), f32), V((2, 16, 1024), bf16), V((16, 2, 16, 1024), bf16),
            V((2, 64, 256), bf16), V((2, 64, 256), f32), V((2, 64, 256), bf16), V((2, 64, 256), bf16),
            V((16, 144, 256), bf16),
            V((3, 128, 256), f32), V((3, 128, 256), f32), V((128, 768), bf16),
            V((4, 64, 256), f32), V((8, 128, 256), bf16), V((8, 128, 256), bf16),
            V((4, 64, 256), bf16), V((4, 64, 256), bf16), V((4, 64, 256), bf16), V((4, 64, 256), bf16),
            V((4, 64, 256), bf16), V((4, 64, 256), bf16), V((4, 64, 256), bf16), V((4, 64, 256), bf16),
            S((16,)), S((16,)), S((16,)), S((16,)), S((3,)), S((3,)), S((24,)), S((24,)),
        ],
        compiler_params=pltpu.CompilerParams(
            collective_id=0, has_side_effects=True, vmem_limit_bytes=62 * 1024 * 1024
        ),
    )(
        query, keys, values, lengths, residual, out_proj, norm_gain, expert_ids.T,
        gate_scores.T, w_gate[0], w_up[0], w_down[0],
    )
    return (out[0].astype(bf16), out[1].astype(bf16))


def solution(mesh):
    in_specs = (
        P(("expert", "tensor"), None),
        P(("expert", "tensor"), None, None, None),
        P(("expert", "tensor"), None, None, None),
        P(("expert", "tensor")),
        P("tensor", "expert"),
        P("expert", "tensor"),
        P("expert"),
        P(),
        P(),
        P("expert", "tensor", None),
        P("expert", "tensor", None),
        P("expert", "tensor", None),
    )
    out_specs = (P("tensor", "expert"), P("tensor", "expert"))
    fused = dict(mesh.shape) == {"expert": 16, "tensor": 2}
    return jax.shard_map(fused_body if fused else body, mesh=mesh, in_specs=in_specs, out_specs=out_specs, check_vma=False)
```

```python
import jax
import jax.numpy as jnp
from jax import lax
from jax.experimental import pallas as pl
from jax.experimental.pallas import tpu as pltpu
from jax.sharding import PartitionSpec as P

floor_value = -1e30
epsilon = 1e-06


def softmax_parts(queries, key_block, value_block, usable, score_scale):
    scores = (
        jnp.einsum("rkgd,rpkd->rkgp", queries, key_block, preferred_element_type=jnp.float32)
        * score_scale
    )
    usable_mask = usable[:, None, None, :]
    peak = jnp.max(jnp.where(usable_mask, scores, floor_value), axis=-1)
    raw_weights = jnp.where(usable_mask, jnp.exp(scores - peak[..., None]), 0.0)
    weight_sum = jnp.sum(raw_weights, axis=-1)
    weighted = jnp.einsum("rkgp,rpkd->rkgd", raw_weights, value_block.astype(jnp.float32))
    return (weight_sum, weighted)


def body(
    query,
    cache_keys,
    cache_values,
    lengths,
    residual,
    out_proj,
    norm_gain,
    expert_ids,
    gate_scores,
    w_gate,
    w_up,
    w_down,
):
    row_count, full_heads_width = query.shape
    cache_len = cache_keys.shape[1]
    kv_count = cache_keys.shape[2]
    head_size = cache_keys.shape[3]
    head_count = full_heads_width // head_size
    group_size = head_count // kv_count
    score_scale = head_size ** (-0.5)
    usable = jnp.arange(cache_len, dtype=jnp.int32)[None, :] < lengths[:, None]
    grouped = query.reshape(row_count, kv_count, group_size, head_size)
    weight_sum, weighted = softmax_parts(grouped, cache_keys, cache_values, usable, score_scale)
    context_rows_own = (
        (weighted / weight_sum[..., None]).astype(jnp.bfloat16).reshape(row_count, full_heads_width)
    )
    context = lax.all_to_all(context_rows_own, "tensor", split_axis=1, concat_axis=0, tiled=True)
    attn_part = jnp.dot(
        lax.all_gather(context, "expert", axis=0, tiled=True),
        out_proj.T,
        preferred_element_type=jnp.float32,
    )
    attn_share = lax.psum_scatter(attn_part, "tensor", scatter_dimension=0, tiled=True)
    hidden_state = residual.astype(jnp.float32) + attn_share
    squares = lax.psum(jnp.sum(hidden_state * hidden_state, axis=1), "expert")
    full_width = hidden_state.shape[1] * lax.axis_size("expert")
    scaled_share = (hidden_state * norm_gain.astype(jnp.float32)[None, :]).astype(jnp.bfloat16)
    scaled = lax.all_gather(
        lax.all_gather(scaled_share, "tensor", axis=0, tiled=True), "expert", axis=1, tiled=True
    )
    mean_all = lax.all_gather(squares / full_width, "tensor", axis=0, tiled=True)
    row_scale = lax.rsqrt(mean_all + epsilon)[:, None]
    experts_local = w_gate.shape[0]
    gate_weight = gate_scores.astype(jnp.float32)
    gate_weight = gate_weight / jnp.sum(gate_weight, axis=1, keepdims=True)
    mixed = None
    for local in range(experts_local):
        expert = lax.axis_index("expert") * experts_local + local
        weight = jnp.sum(jnp.where(expert_ids == expert, gate_weight, 0.0), axis=1, keepdims=True)
        gate_proj = row_scale * lax.dot_general(
            scaled, w_gate[local], (((1,), (1,)), ((), ())), preferred_element_type=jnp.float32
        )
        up_proj = row_scale * lax.dot_general(
            scaled, w_up[local], (((1,), (1,)), ((), ())), preferred_element_type=jnp.float32
        )
        activation = (jax.nn.silu(gate_proj) * up_proj).astype(jnp.bfloat16)
        part = weight * jnp.dot(activation, w_down[local], preferred_element_type=jnp.float32)
        mixed = part if mixed is None else mixed + part
    mixed = lax.psum_scatter(
        mixed.astype(jnp.bfloat16), "tensor", scatter_dimension=0, tiled=True
    )
    mixed_share = lax.psum_scatter(mixed, "expert", scatter_dimension=1, tiled=True)
    return (hidden_state.astype(jnp.bfloat16), mixed_share)


MESH = pl.DeviceIdType.MESH
NZ = 4
ACROSS, CORE = 4, 8


def remote(src, dst, send, recv, device):
    return pltpu.make_async_remote_copy(
        src_ref=src, dst_ref=dst, send_sem=send, recv_sem=recv, device_id=device, device_id_type=MESH
    )


class Net:
    def __init__(self, buf, sends, recvs, place, order):
        self.buf, self.sends, self.recvs = buf, sends, recvs
        self.z, self.x, self.c, self.y = place
        self.order = order
        self.started = []

    def slot(self, zz, xx, cc):
        return zz * 4 + xx * 2 + cc

    def copy(self, slot, half, send, recv, device):
        ref = self.buf.at[slot] if half is None else self.buf.at[slot, half]
        return remote(ref, ref, self.sends.at[send], self.recvs.at[recv], device)

    def go(self, slot, half, send, recv, device):
        copy = self.copy(slot, half, send, recv, device)
        copy.start()
        self.started.append(copy)

    def landed(self, slot, half, recv):
        e = self.slot(self.z, self.x, self.c)
        self.copy(slot, half, 0, recv, (e, 1 - self.y)).wait_recv()

    def along_z(self, half, base):
        z, x, c = self.z, self.x, self.c
        for i in range(NZ - 1):
            zz = self.order[i]
            self.go(self.slot(z, x, c), half, base + zz, base + z, (self.slot(zz, x, c), self.y))

    def z_landed(self, zz, half, base):
        self.landed(self.slot(zz, self.x, self.c), half, base + zz)

    def to_core(self, zz, xx, half, base):
        sem = base + xx * NZ + zz
        other = (self.slot(self.z, self.x, 1 - self.c), self.y)
        self.go(self.slot(zz, xx, self.c), half, sem, sem, other)

    def core_landed(self, zz, xx, half, base):
        self.landed(self.slot(zz, xx, 1 - self.c), half, base + xx * NZ + zz)

    def wait_sends(self):
        for copy in self.started:
            copy.wait_send()


class PlaneGather(Net):
    def onward(self, zz, k):
        half, sem = self.halves[k], 8 + k * NZ + zz
        z, x, c = self.z, self.x, self.c
        self.go(self.slot(zz, x, c), half, sem, sem, (self.slot(z, 1 - x, c), self.y))
        self.to_core(zz, x, half, 16 + 8 * k)

    def take_z(self, i, k):
        zz = self.order[NZ - 1 - i]
        self.z_landed(zz, self.halves[k], k * NZ)
        self.onward(zz, k)

    def take_x(self, i, k):
        zz = self.order[NZ - 1 - i]
        self.landed(self.slot(zz, 1 - self.x, self.c), self.halves[k], 8 + k * NZ + zz)
        self.to_core(zz, 1 - self.x, self.halves[k], 16 + 8 * k)

    def run(self, swap):
        z = self.z
        self.halves = (self.y, 1 - self.y)
        self.along_z(self.halves[0], 0)
        self.onward(z, 0)
        swap.wait_recv()
        self.along_z(self.halves[1], NZ)
        self.onward(z, 1)
        for i in range(1, NZ):
            self.take_z(i, 0)
        self.take_x(0, 0)
        for i in range(1, NZ):
            self.take_z(i, 1)
        for i in range(1, NZ):
            self.take_x(i, 0)
        for i in range(NZ):
            self.take_x(i, 1)

    def wait_core(self):
        for zz in range(NZ):
            for xx in range(2):
                for k in range(2):
                    self.core_landed(zz, xx, self.halves[k], 16 + 8 * k)


class QuadGather(Net):
    def onward(self, zz):
        z, x, c, y = self.z, self.x, self.c, self.y
        own, across = self.slot(z, x, c), self.slot(z, 1 - x, c)
        src = self.slot(zz, x, c)
        self.go(src, y, 4 + zz, 4 + zz, (across, 1 - y))
        self.go(src, y, 8 + zz, 8 + zz, (across, y))
        self.go(src, y, 12 + zz, 12 + zz, (own, 1 - y))

    def begin(self):
        self.along_z(self.y, 0)
        self.onward(self.z)

    def take_z(self, i):
        zz = self.order[NZ - 1 - i]
        self.z_landed(zz, self.y, 0)
        self.onward(zz)

    def take_level(self, i):
        zz = self.order[NZ - 1 - i]
        near, far = self.slot(zz, self.x, self.c), self.slot(zz, 1 - self.x, self.c)
        self.landed(near, 1 - self.y, 12 + zz)
        self.to_core(zz, self.x, None, 16)
        self.landed(far, self.y, 8 + zz)
        self.landed(far, 1 - self.y, 4 + zz)
        self.to_core(zz, 1 - self.x, None, 16)
        return [near, far]

    def take_core(self, i):
        zz = self.order[NZ - 1 - i]
        for xx in (self.x, 1 - self.x):
            self.core_landed(zz, xx, None, 16)
        return [self.slot(zz, self.x, 1 - self.c), self.slot(zz, 1 - self.x, 1 - self.c)]


def nt_dot(a, b):
    return lax.dot_general(a, b, (((1,), (1,)), ((), ())), preferred_element_type=jnp.float32)


def layer_kernel(
    q_hbm, k_hbm, v_hbm, len_ref, res_hbm, wo_hbm, gain_hbm, ids_hbm, gates_hbm,
    wg_hbm, wu_hbm, wd_hbm,
    out_ref,
    q_ref, res_ref, gain_ref, ids_ref, gates_ref,
    k_v, v_v, wo_v, wg_v, wu_v, wd_v, local_sems,
    lay, qlay, sblk, ctx, part, part_out, part_in, hid_all,
    gate_acc, up_acc, act, mine, core_out, core_in, x_out, x_in, y_out, y_in, d_out, d_in, z_out, z_in,
    c_send, c_recv, h_send, h_recv, p_send, p_recv, r_send, r_recv,
):
    f32, bf16 = jnp.float32, jnp.bfloat16
    e = lax.axis_index("expert")
    y = lax.axis_index("tensor")
    z, x, c = e // 4, (e // 2) % 2, e % 2
    ex, ec = e + 2 * (1 - 2 * x), e + 1 - 2 * c
    mirror = z // 2
    near_z = z + mirror * (3 - 2 * z)
    order = [o + mirror * (3 - 2 * o) for o in (3, 2, 1 - near_z, near_z)]
    barrier = pltpu.get_barrier_semaphore()
    pairs = [(k_hbm, k_v), (v_hbm, v_v), (wo_hbm, wo_v), (wg_hbm, wg_v), (wu_hbm, wu_v), (wd_hbm, wd_v)]
    pairs += [(q_hbm, q_ref), (res_hbm, res_ref), (gain_hbm, gain_ref), (ids_hbm, ids_ref), (gates_hbm, gates_ref)]
    loads = [pltpu.make_async_copy(s, d, local_sems.at[i]) for i, (s, d) in enumerate(pairs)]
    first = [loads[6], loads[0], loads[1]]
    for d in first:
        d.start()
    peers = [(ec, y), (ex, y), (e, 1 - y), (ex, 1 - y)]
    peers += [(order[i] * 4 + x * 2 + c, y) for i in range(NZ - 1)]
    for dev in peers:
        pl.semaphore_signal(barrier, inc=1, device_id=dev, device_id_type=MESH)

    rows = q_ref.shape[0]
    col = lax.broadcasted_iota(jnp.int32, (64, 512), 1)
    head = lax.broadcasted_iota(jnp.int32, (64, 512), 0)
    same = (col % 4) == (head // 16)
    loads[6].wait()
    for h in range(64):
        qlay[h * 8 : h * 8 + rows, :] = q_ref[:, h * 128 : (h + 1) * 128].astype(f32)
    loads[0].wait()
    loads[1].wait()
    for d in loads[2:6] + loads[7:]:
        d.start()
    for r in range(rows):
        q = qlay[pl.ds(r, 64, stride=8), :].astype(bf16)
        s = nt_dot(q, k_v[r]) * (128 ** -0.5)
        ok = same & ((col // 4) < len_ref[r])
        peak = jnp.max(jnp.where(ok, s, -1e30), axis=1, keepdims=True)
        w = jnp.where(ok, jnp.exp(s - peak), 0.0)
        total = jnp.sum(w, axis=1, keepdims=True)
        o = jnp.dot(w.astype(bf16), v_v[r], preferred_element_type=f32) / total
        for half in range(2):
            for j in range(4):
                h0 = half * 32 + j * 8
                lay[pl.ds(half * 128 + 4 * j + r, 8, stride=16), :] = o[h0 : h0 + 8]
    for half in range(2):
        for hh in range(8):
            t = (half * 8 + hh) * 16
            sblk[half, :, hh * 128 : (hh + 1) * 128] = lay[t : t + 16, :].astype(bf16)
    ctx[e, y] = sblk[y]
    pl.semaphore_wait(barrier, 7)

    swap = remote(sblk.at[1 - y], ctx.at[e, y], p_send.at[0], p_recv.at[0], (e, 1 - y))
    swap.start()
    g1 = PlaneGather(ctx, c_send, c_recv, (z, x, c, y), order)
    g1.run(swap)
    g1.wait_core()

    loads[2].wait()
    lhs = ctx.reshape(512, 1024)
    quarter = (lax.broadcasted_iota(jnp.int32, (512, 256), 0) % 16) // 4
    acc = jnp.zeros((512, 256), f32)
    for j in range(4):
        pj = nt_dot(lhs[...], wo_v[:, j * 1024 : (j + 1) * 1024])
        acc = jnp.where(quarter == j, pj, acc)
    folded = acc.reshape(32, 2, 8, 256)
    folded = (folded[:, 0] + folded[:, 1]).reshape(256, 256)
    low = (lax.broadcasted_iota(jnp.int32, (256, 256), 0) % 8) < 4
    folded = folded + jnp.where(low, pltpu.roll(folded, 252, 0), pltpu.roll(folded, 4, 0))
    folded = folded.reshape(16, 2, 8, 256)
    low3 = lax.broadcasted_iota(jnp.int32, (16, 8, 256), 1) < 4
    part[...] = jnp.where(low3, folded[:, 0], folded[:, 1]).reshape(2, 64, 256)
    part_out[...] = part[1 - y].astype(bf16)
    psend = remote(part_out, part_in, p_send.at[1], p_recv.at[1], (e, 1 - y))
    psend.start()
    for d in loads[7:]:
        d.wait()
    psend.wait_recv()
    hidden = res_ref[...].astype(f32) + (part[y] + part_in[...].astype(f32))
    hid_all[e, y, 0:64] = (hidden * gain_ref[...].astype(f32).reshape(1, 256)).astype(bf16)
    ss = jnp.sum(hidden * hidden, axis=1, keepdims=True)
    spot = lax.broadcasted_iota(jnp.int32, (64, 128), 0) + 64 * y
    lane = lax.broadcasted_iota(jnp.int32, (64, 128), 1)
    sq = jnp.sum(jnp.where(spot == lane, ss, 0.0), axis=0, keepdims=True)
    sq_high = sq.astype(bf16).astype(f32)
    hid_all[e, y, 64:80, 0:128] = jnp.broadcast_to(sq_high, (16, 128)).astype(bf16)
    hid_all[e, y, 64:80, 128:256] = jnp.broadcast_to(sq - sq_high, (16, 128)).astype(bf16)
    g2 = QuadGather(hid_all, h_send, h_recv, (z, x, c, y), order)
    g2.begin()
    out_ref[0] = hidden
    eye = lax.broadcasted_iota(jnp.int32, (128, 128), 0) == lax.broadcasted_iota(jnp.int32, (128, 128), 1)
    gw = gates_ref[...].astype(f32)
    gw = gw / jnp.sum(gw, axis=0, keepdims=True)
    weight_row = jnp.sum(jnp.where(ids_ref[...] == e, gw, 0.0), axis=0, keepdims=True)
    weight = jnp.sum(jnp.where(eye, weight_row, 0.0), axis=1, keepdims=True)

    def products(slots, first=False):
        for n in range(3):
            for wref, aref in ((wg_v, gate_acc), (wu_v, up_acc)):
                a = None if first else aref[n]
                for src in slots:
                    cols = pl.ds(pl.multiple_of(src * 256, 256), 256)
                    t = nt_dot(hid_all[src, :, 0:64].reshape(128, 256), wref[n * 256 : (n + 1) * 256, cols])
                    a = t if a is None else a + t
                aref[n] = a

    for i in range(1, NZ):
        g2.take_z(i)
    loads[3].wait()
    loads[4].wait()
    products(g2.take_level(0), True)
    for i in range(1, NZ):
        products(g2.take_level(i) + g2.take_core(i - 1))
    products(g2.take_core(NZ - 1))

    tail = jnp.sum(hid_all[:, :, 64:80, :].reshape(32, 16, 256).astype(f32), axis=0)[0:1]
    scale_row = lax.rsqrt((tail[:, 0:128] + tail[:, 128:256]) / 4096.0 + epsilon)
    scale = jnp.sum(jnp.where(eye, scale_row, 0.0), axis=1, keepdims=True)
    for n in range(3):
        g = gate_acc[n] * scale
        u = up_acc[n] * scale
        a = (g / (1.0 + jnp.exp(-g)) * u * weight).astype(bf16)
        for half in range(2):
            to = pl.ds(pl.multiple_of(((half + y) % 2) * 64, 64), 64)
            act[to, n * 256 : (n + 1) * 256] = a[half * 64 : (half + 1) * 64]
    loads[5].wait()

    def block(zz, xx, cc):
        cols = pl.ds(pl.multiple_of((zz * 4 + xx * 2 + cc) * 256, 256), 256)
        return jnp.dot(act[...], wd_v[:, cols], preferred_element_type=f32)

    def core_copy(zz, k):
        b = k * NZ + zz
        return remote(core_out.at[b], core_in.at[b], r_send.at[b], r_recv.at[b], (ec, y))

    def x_copy(zz):
        return remote(x_out.at[zz], x_in.at[zz], r_send.at[8 + zz], r_recv.at[8 + zz], (ex, y))

    def y_copy(zz):
        return remote(y_out.at[zz], y_in.at[zz], r_send.at[12 + zz], r_recv.at[12 + zz], (e, 1 - y))

    def d_copy(zz):
        return remote(d_out.at[zz], d_in.at[zz], r_send.at[16 + zz], r_recv.at[16 + zz], (ex, 1 - y))

    def z_copy(zz):
        return remote(
            z_out.at[zz], z_in.at[z], r_send.at[20 + zz], r_recv.at[20 + z], (zz * 4 + x * 2 + c, y)
        )

    def z_landing(zz):
        return remote(
            z_out.at[zz], z_in.at[zz], r_send.at[20 + z], r_recv.at[20 + zz], (zz * 4 + x * 2 + c, y)
        )

    def to_core(zz):
        for k, xx in enumerate((1 - x, x)):
            core_out[k * NZ + zz] = block(zz, xx, 1 - c).astype(bf16)
            core_copy(zz, k).start()

    def to_plane(zz):
        far = block(zz, 1 - x, c)
        core_copy(zz, 0).wait_recv()
        far = far + core_in[zz].astype(f32)
        d_out[zz] = far[64:128].astype(bf16)
        d_copy(zz).start()
        x_out[zz] = far[0:64].astype(bf16)
        x_copy(zz).start()
        near = block(zz, x, c)
        core_copy(zz, 1).wait_recv()
        near = near + core_in[NZ + zz].astype(f32)
        y_out[zz] = near[64:128].astype(bf16)
        y_copy(zz).start()
        mine[zz] = near[0:64]

    def plane_sum(zz):
        x_copy(zz).wait_recv()
        y_copy(zz).wait_recv()
        d_copy(zz).wait_recv()
        return mine[zz] + x_in[zz].astype(f32) + (y_in[zz].astype(f32) + d_in[zz].astype(f32))

    to_core(order[0])
    for i in range(NZ):
        if i < NZ - 1:
            to_core(order[i + 1])
        to_plane(order[i])
    for i in range(NZ - 1):
        zz = order[i]
        z_out[zz] = plane_sum(zz).astype(bf16)
        z_copy(zz).start()
    fin = plane_sum(z)
    for i in range(NZ - 2, -1, -1):
        zz = order[i]
        z_landing(zz).wait_recv()
        fin = fin + z_in[zz].astype(f32)
    out_ref[1] = fin

    for d in (swap, psend):
        d.wait_send()
    g1.wait_sends()
    g2.wait_sends()
    for i in range(NZ):
        zz = order[i]
        core_copy(zz, 0).wait_send()
        core_copy(zz, 1).wait_send()
        x_copy(zz).wait_send()
        y_copy(zz).wait_send()
        d_copy(zz).wait_send()
        if i < NZ - 1:
            z_copy(zz).wait_send()


def fused_body(
    query, cache_keys, cache_values, lengths, residual, out_proj, norm_gain, expert_ids, gate_scores,
    w_gate, w_up, w_down,
):
    f32, bf16 = jnp.float32, jnp.bfloat16
    rows = query.shape[0]
    keys = cache_keys.reshape(rows, 512, 128)
    values = cache_values.reshape(rows, 512, 128)
    vm = pl.BlockSpec(memory_space=pltpu.VMEM)
    hb = pl.BlockSpec(memory_space=pl.ANY)
    sm = pl.BlockSpec(memory_space=pltpu.SMEM)
    V, S = pltpu.VMEM, pltpu.SemaphoreType.DMA
    out = pl.pallas_call(
        layer_kernel,
        name="layer",
        out_shape=jax.ShapeDtypeStruct((2, 64, 256), f32),
        in_specs=[hb, hb, hb, sm, hb, hb, hb, hb, hb, hb, hb, hb],
        out_specs=vm,
        scratch_shapes=[
            V((rows, 8192), bf16), V((64, 256), bf16), V((256,), bf16), V((8, 128), jnp.int32), V((8, 128), bf16),
            V((rows, 512, 128), bf16), V((rows, 512, 128), bf16), V((256, 4096), bf16),
            V((768, 4096), bf16), V((768, 4096), bf16), V((768, 4096), bf16), S((11,)),
            V((256, 128), f32), V((512, 128), f32), V((2, 16, 1024), bf16), V((16, 2, 16, 1024), bf16),
            V((2, 64, 256), f32), V((64, 256), bf16), V((64, 256), bf16),
            V((16, 2, 80, 256), bf16),
            V((3, 128, 256), f32), V((3, 128, 256), f32), V((128, 768), bf16),
            V((4, 64, 256), f32), V((8, 128, 256), bf16), V((8, 128, 256), bf16),
            V((4, 64, 256), bf16), V((4, 64, 256), bf16), V((4, 64, 256), bf16), V((4, 64, 256), bf16),
            V((4, 64, 256), bf16), V((4, 64, 256), bf16), V((4, 64, 256), bf16), V((4, 64, 256), bf16),
            S((32,)), S((32,)), S((24,)), S((24,)), S((2,)), S((2,)), S((24,)), S((24,)),
        ],
        compiler_params=pltpu.CompilerParams(
            collective_id=0, has_side_effects=True, vmem_limit_bytes=62 * 1024 * 1024
        ),
    )(
        query, keys, values, lengths, residual, out_proj, norm_gain, expert_ids.T,
        gate_scores.T, w_gate[0], w_up[0], w_down[0],
    )
    return (out[0].astype(bf16), out[1].astype(bf16))


def solution(mesh):
    in_specs = (
        P(("expert", "tensor"), None),
        P(("expert", "tensor"), None, None, None),
        P(("expert", "tensor"), None, None, None),
        P(("expert", "tensor")),
        P("tensor", "expert"),
        P("expert", "tensor"),
        P("expert"),
        P(),
        P(),
        P("expert", "tensor", None),
        P("expert", "tensor", None),
        P("expert", "tensor", None),
    )
    out_specs = (P("tensor", "expert"), P("tensor", "expert"))
    fused = dict(mesh.shape) == {"expert": 16, "tensor": 2}
    return jax.shard_map(fused_body if fused else body, mesh=mesh, in_specs=in_specs, out_specs=out_specs, check_vma=False)
```

```python
import jax
import jax.numpy as jnp
from jax import lax
from jax.experimental import pallas as pl
from jax.experimental.pallas import tpu as pltpu
from jax.sharding import PartitionSpec as P

floor_value = -1e30
epsilon = 1e-06


def softmax_parts(queries, key_block, value_block, usable, score_scale):
    scores = (
        jnp.einsum("rkgd,rpkd->rkgp", queries, key_block, preferred_element_type=jnp.float32)
        * score_scale
    )
    usable_mask = usable[:, None, None, :]
    peak = jnp.max(jnp.where(usable_mask, scores, floor_value), axis=-1)
    raw_weights = jnp.where(usable_mask, jnp.exp(scores - peak[..., None]), 0.0)
    weight_sum = jnp.sum(raw_weights, axis=-1)
    weighted = jnp.einsum("rkgp,rpkd->rkgd", raw_weights, value_block.astype(jnp.float32))
    return (weight_sum, weighted)


def body(
    query,
    cache_keys,
    cache_values,
    lengths,
    residual,
    out_proj,
    norm_gain,
    expert_ids,
    gate_scores,
    w_gate,
    w_up,
    w_down,
):
    row_count, full_heads_width = query.shape
    cache_len = cache_keys.shape[1]
    kv_count = cache_keys.shape[2]
    head_size = cache_keys.shape[3]
    head_count = full_heads_width // head_size
    group_size = head_count // kv_count
    score_scale = head_size ** (-0.5)
    usable = jnp.arange(cache_len, dtype=jnp.int32)[None, :] < lengths[:, None]
    grouped = query.reshape(row_count, kv_count, group_size, head_size)
    weight_sum, weighted = softmax_parts(grouped, cache_keys, cache_values, usable, score_scale)
    context_rows_own = (
        (weighted / weight_sum[..., None]).astype(jnp.bfloat16).reshape(row_count, full_heads_width)
    )
    context = lax.all_to_all(context_rows_own, "tensor", split_axis=1, concat_axis=0, tiled=True)
    attn_part = jnp.dot(
        lax.all_gather(context, "expert", axis=0, tiled=True),
        out_proj.T,
        preferred_element_type=jnp.float32,
    )
    attn_share = lax.psum_scatter(attn_part, "tensor", scatter_dimension=0, tiled=True)
    hidden_state = residual.astype(jnp.float32) + attn_share
    squares = lax.psum(jnp.sum(hidden_state * hidden_state, axis=1), "expert")
    full_width = hidden_state.shape[1] * lax.axis_size("expert")
    scaled_share = (hidden_state * norm_gain.astype(jnp.float32)[None, :]).astype(jnp.bfloat16)
    scaled = lax.all_gather(
        lax.all_gather(scaled_share, "tensor", axis=0, tiled=True), "expert", axis=1, tiled=True
    )
    mean_all = lax.all_gather(squares / full_width, "tensor", axis=0, tiled=True)
    row_scale = lax.rsqrt(mean_all + epsilon)[:, None]
    experts_local = w_gate.shape[0]
    gate_weight = gate_scores.astype(jnp.float32)
    gate_weight = gate_weight / jnp.sum(gate_weight, axis=1, keepdims=True)
    mixed = None
    for local in range(experts_local):
        expert = lax.axis_index("expert") * experts_local + local
        weight = jnp.sum(jnp.where(expert_ids == expert, gate_weight, 0.0), axis=1, keepdims=True)
        gate_proj = row_scale * lax.dot_general(
            scaled, w_gate[local], (((1,), (1,)), ((), ())), preferred_element_type=jnp.float32
        )
        up_proj = row_scale * lax.dot_general(
            scaled, w_up[local], (((1,), (1,)), ((), ())), preferred_element_type=jnp.float32
        )
        activation = (jax.nn.silu(gate_proj) * up_proj).astype(jnp.bfloat16)
        part = weight * jnp.dot(activation, w_down[local], preferred_element_type=jnp.float32)
        mixed = part if mixed is None else mixed + part
    mixed = lax.psum_scatter(
        mixed.astype(jnp.bfloat16), "tensor", scatter_dimension=0, tiled=True
    )
    mixed_share = lax.psum_scatter(mixed, "expert", scatter_dimension=1, tiled=True)
    return (hidden_state.astype(jnp.bfloat16), mixed_share)


MESH = pl.DeviceIdType.MESH
NZ = 4
ACROSS, CORE = 4, 8


def remote(src, dst, send, recv, device):
    return pltpu.make_async_remote_copy(
        src_ref=src, dst_ref=dst, send_sem=send, recv_sem=recv, device_id=device, device_id_type=MESH
    )


class Net:
    def __init__(self, buf, sends, recvs, place, order):
        self.buf, self.sends, self.recvs = buf, sends, recvs
        self.z, self.x, self.c, self.y = place
        self.order = order
        self.started = []

    def slot(self, zz, xx, cc):
        return zz * 4 + xx * 2 + cc

    def copy(self, slot, half, send, recv, device):
        ref = self.buf.at[slot] if half is None else self.buf.at[slot, half]
        return remote(ref, ref, self.sends.at[send], self.recvs.at[recv], device)

    def go(self, slot, half, send, recv, device):
        copy = self.copy(slot, half, send, recv, device)
        copy.start()
        self.started.append(copy)

    def landed(self, slot, half, recv):
        e = self.slot(self.z, self.x, self.c)
        self.copy(slot, half, 0, recv, (e, 1 - self.y)).wait_recv()

    def along_z(self, half, base):
        z, x, c = self.z, self.x, self.c
        for i in range(NZ - 2, -1, -1):
            zz = self.order[i]
            self.go(self.slot(z, x, c), half, base + zz, base + z, (self.slot(zz, x, c), self.y))

    def z_landed(self, zz, half, base):
        self.landed(self.slot(zz, self.x, self.c), half, base + zz)

    def to_core(self, zz, xx, half, base):
        sem = base + xx * NZ + zz
        other = (self.slot(self.z, self.x, 1 - self.c), self.y)
        self.go(self.slot(zz, xx, self.c), half, sem, sem, other)

    def core_landed(self, zz, xx, half, base):
        self.landed(self.slot(zz, xx, 1 - self.c), half, base + xx * NZ + zz)

    def wait_sends(self):
        for copy in self.started:
            copy.wait_send()


class PlaneGather(Net):
    def onward(self, zz, k):
        half, sem = self.halves[k], 8 + k * NZ + zz
        z, x, c = self.z, self.x, self.c
        self.go(self.slot(zz, x, c), half, sem, sem, (self.slot(z, 1 - x, c), self.y))
        self.to_core(zz, x, half, 16 + 8 * k)

    def take_z(self, i, k):
        zz = self.order[NZ - 1 - i]
        self.z_landed(zz, self.halves[k], k * NZ)
        self.onward(zz, k)

    def take_x(self, i, k):
        zz = self.order[NZ - 1 - i]
        self.landed(self.slot(zz, 1 - self.x, self.c), self.halves[k], 8 + k * NZ + zz)
        self.to_core(zz, 1 - self.x, self.halves[k], 16 + 8 * k)

    def run(self, swap):
        z = self.z
        self.halves = (self.y, 1 - self.y)
        self.along_z(self.halves[0], 0)
        self.onward(z, 0)
        swap.wait_recv()
        self.along_z(self.halves[1], NZ)
        self.onward(z, 1)
        for i in range(1, NZ):
            self.take_z(i, 0)
        self.take_x(0, 0)
        for i in range(1, NZ):
            self.take_z(i, 1)
        for i in range(1, NZ):
            self.take_x(i, 0)
        for i in range(NZ):
            self.take_x(i, 1)

    def wait_core(self):
        for zz in range(NZ):
            for xx in range(2):
                for k in range(2):
                    self.core_landed(zz, xx, self.halves[k], 16 + 8 * k)


class QuadGather(Net):
    def onward(self, zz):
        z, x, c, y = self.z, self.x, self.c, self.y
        own, across = self.slot(z, x, c), self.slot(z, 1 - x, c)
        src = self.slot(zz, x, c)
        self.go(src, y, 4 + zz, 4 + zz, (across, 1 - y))
        self.go(src, y, 8 + zz, 8 + zz, (across, y))
        self.go(src, y, 12 + zz, 12 + zz, (own, 1 - y))

    def begin(self):
        self.along_z(self.y, 0)
        self.onward(self.z)

    def take_z(self, i):
        zz = self.order[NZ - 1 - i]
        self.z_landed(zz, self.y, 0)
        self.onward(zz)

    def take_level(self, i):
        zz = self.order[NZ - 1 - i]
        near, far = self.slot(zz, self.x, self.c), self.slot(zz, 1 - self.x, self.c)
        self.landed(near, 1 - self.y, 12 + zz)
        self.to_core(zz, self.x, None, 16)
        self.landed(far, self.y, 8 + zz)
        self.landed(far, 1 - self.y, 4 + zz)
        self.to_core(zz, 1 - self.x, None, 16)
        return [near, far]

    def take_core(self, i):
        zz = self.order[NZ - 1 - i]
        for xx in (self.x, 1 - self.x):
            self.core_landed(zz, xx, None, 16)
        return [self.slot(zz, self.x, 1 - self.c), self.slot(zz, 1 - self.x, 1 - self.c)]


def nt_dot(a, b):
    return lax.dot_general(a, b, (((1,), (1,)), ((), ())), preferred_element_type=jnp.float32)


def layer_kernel(
    q_hbm, k_hbm, v_hbm, len_ref, res_hbm, wo_hbm, gain_hbm, ids_hbm, gates_hbm,
    wg_hbm, wu_hbm, wd_hbm,
    out_ref,
    q_ref, res_ref, gain_ref, ids_ref, gates_ref,
    k_v, v_v, wo_v, wg_v, wu_v, wd_v, local_sems,
    lay, qlay, sblk, ctx, part_out, part_in, hid_all,
    gate_acc, up_acc, act, mine, core_out, core_in, x_out, x_in, y_out, y_in, d_out, d_in, z_out, z_in,
    c_send, c_recv, h_send, h_recv, p_send, p_recv, r_send, r_recv,
):
    f32, bf16 = jnp.float32, jnp.bfloat16
    e = lax.axis_index("expert")
    y = lax.axis_index("tensor")
    z, x, c = e // 4, (e // 2) % 2, e % 2
    ex, ec = e + 2 * (1 - 2 * x), e + 1 - 2 * c
    mirror = z // 2
    near_z = z + mirror * (3 - 2 * z)
    order = [o + mirror * (3 - 2 * o) for o in (3, 2, 1 - near_z, near_z)]
    barrier = pltpu.get_barrier_semaphore()
    pairs = [(k_hbm, k_v), (v_hbm, v_v), (wo_hbm, wo_v), (wg_hbm, wg_v), (wu_hbm, wu_v), (wd_hbm, wd_v)]
    pairs += [(q_hbm, q_ref), (res_hbm, res_ref), (gain_hbm, gain_ref), (ids_hbm, ids_ref), (gates_hbm, gates_ref)]
    loads = [pltpu.make_async_copy(s, d, local_sems.at[i]) for i, (s, d) in enumerate(pairs)]
    first = [loads[6], loads[0], loads[1]]
    for d in first:
        d.start()
    peers = [(ec, y), (ex, y), (e, 1 - y), (ex, 1 - y)]
    peers += [(order[i] * 4 + x * 2 + c, y) for i in range(NZ - 1)]
    for dev in peers:
        pl.semaphore_signal(barrier, inc=1, device_id=dev, device_id_type=MESH)

    rows = q_ref.shape[0]
    col = lax.broadcasted_iota(jnp.int32, (64, 512), 1)
    head = lax.broadcasted_iota(jnp.int32, (64, 512), 0)
    same = (col % 4) == (head // 16)
    loads[6].wait()
    for h in range(64):
        qlay[h * 8 : h * 8 + rows, :] = q_ref[:, h * 128 : (h + 1) * 128].astype(f32)
    loads[0].wait()
    loads[1].wait()
    for d in loads[2:6] + loads[7:]:
        d.start()
    scores, weights, totals = [], [], []
    for r in range(rows):
        q = qlay[pl.ds(r, 64, stride=8), :].astype(bf16)
        s = nt_dot(q, k_v[r]) * (128 ** -0.5)
        scores.append(jnp.where(same & ((col // 4) < len_ref[r]), s, -1e30))
    for s in scores:
        w = jnp.exp(s - jnp.max(s, axis=1, keepdims=True))
        totals.append(jnp.sum(w, axis=1, keepdims=True))
        weights.append(w.astype(bf16))
    for r in range(rows):
        o = jnp.dot(weights[r], v_v[r], preferred_element_type=f32) / totals[r]
        for half in range(2):
            for j in range(4):
                h0 = half * 32 + j * 8
                lay[pl.ds(half * 128 + 4 * j + r, 8, stride=16), :] = o[h0 : h0 + 8]
    for half in range(2):
        for hh in range(8):
            t = (half * 8 + hh) * 16
            sblk[half, :, hh * 128 : (hh + 1) * 128] = lay[t : t + 16, :].astype(bf16)
    ctx[e, y] = sblk[y]
    pl.semaphore_wait(barrier, 7)

    swap = remote(sblk.at[1 - y], ctx.at[e, y], p_send.at[0], p_recv.at[0], (e, 1 - y))
    swap.start()
    g1 = PlaneGather(ctx, c_send, c_recv, (z, x, c, y), order)
    g1.run(swap)
    g1.wait_core()

    loads[2].wait()
    quarter = (lax.broadcasted_iota(jnp.int32, (256, 256), 0) % 16) // 4
    low = (lax.broadcasted_iota(jnp.int32, (128, 256), 0) % 8) < 4
    low3 = lax.broadcasted_iota(jnp.int32, (8, 8, 256), 1) < 4

    def attn_half(h):
        lhs = ctx[pl.ds(8 * h, 8)].reshape(256, 1024)
        acc = jnp.zeros((256, 256), f32)
        for j in range(4):
            pj = nt_dot(lhs, wo_v[:, j * 1024 : (j + 1) * 1024])
            acc = jnp.where(quarter == j, pj, acc)
        folded = acc.reshape(16, 2, 8, 256)
        folded = (folded[:, 0] + folded[:, 1]).reshape(128, 256)
        folded = folded + jnp.where(low, pltpu.roll(folded, 124, 0), pltpu.roll(folded, 4, 0))
        folded = folded.reshape(8, 2, 8, 256)
        return jnp.where(low3, folded[:, 0], folded[:, 1]).reshape(64, 256)

    part_out[...] = attn_half(1 - y).astype(bf16)
    psend = remote(part_out, part_in, p_send.at[1], p_recv.at[1], (e, 1 - y))
    psend.start()
    mine_part = attn_half(y)
    for d in loads[7:]:
        d.wait()
    psend.wait_recv()
    hidden = res_ref[...].astype(f32) + (mine_part + part_in[...].astype(f32))
    hid_all[e, y, 0:64] = (hidden * gain_ref[...].astype(f32).reshape(1, 256)).astype(bf16)
    ss = jnp.sum(hidden * hidden, axis=1, keepdims=True)
    spot = lax.broadcasted_iota(jnp.int32, (64, 128), 0) + 64 * y
    lane = lax.broadcasted_iota(jnp.int32, (64, 128), 1)
    sq = jnp.sum(jnp.where(spot == lane, ss, 0.0), axis=0, keepdims=True)
    sq_high = sq.astype(bf16).astype(f32)
    hid_all[e, y, 64:80, 0:128] = jnp.broadcast_to(sq_high, (16, 128)).astype(bf16)
    hid_all[e, y, 64:80, 128:256] = jnp.broadcast_to(sq - sq_high, (16, 128)).astype(bf16)
    g2 = QuadGather(hid_all, h_send, h_recv, (z, x, c, y), order)
    g2.begin()
    swap.wait_send()
    psend.wait_send()
    g1.wait_sends()
    out_ref[0] = hidden.astype(bf16)
    eye = lax.broadcasted_iota(jnp.int32, (128, 128), 0) == lax.broadcasted_iota(jnp.int32, (128, 128), 1)
    gw = gates_ref[...].astype(f32)
    gw = gw / jnp.sum(gw, axis=0, keepdims=True)
    weight_row = jnp.sum(jnp.where(ids_ref[...] == e, gw, 0.0), axis=0, keepdims=True)
    weight = jnp.sum(jnp.where(eye, weight_row, 0.0), axis=1, keepdims=True)

    def products(slots, first=False):
        for n in range(3):
            for wref, aref in ((wg_v, gate_acc), (wu_v, up_acc)):
                a = None if first else aref[n]
                for src in slots:
                    cols = pl.ds(pl.multiple_of(src * 256, 256), 256)
                    t = nt_dot(hid_all[src, :, 0:64].reshape(128, 256), wref[n * 256 : (n + 1) * 256, cols])
                    a = t if a is None else a + t
                aref[n] = a

    for i in range(1, NZ):
        g2.take_z(i)
    loads[3].wait()
    loads[4].wait()
    products(g2.take_level(0), True)
    for i in range(1, NZ):
        products(g2.take_level(i) + g2.take_core(i - 1))
    products(g2.take_core(NZ - 1))

    tail = jnp.sum(hid_all[:, :, 64:80, :].reshape(32, 16, 256).astype(f32), axis=0)[0:1]
    scale_row = lax.rsqrt((tail[:, 0:128] + tail[:, 128:256]) / 4096.0 + epsilon)
    scale = jnp.sum(jnp.where(eye, scale_row, 0.0), axis=1, keepdims=True)
    for n in range(3):
        g = gate_acc[n] * scale
        u = up_acc[n] * scale
        a = (g / (1.0 + jnp.exp(-g)) * u * weight).astype(bf16)
        for half in range(2):
            to = pl.ds(pl.multiple_of(((half + y) % 2) * 64, 64), 64)
            act[to, n * 256 : (n + 1) * 256] = a[half * 64 : (half + 1) * 64]
    loads[5].wait()

    def block(zz, xx, cc):
        cols = pl.ds(pl.multiple_of((zz * 4 + xx * 2 + cc) * 256, 256), 256)
        return jnp.dot(act[...], wd_v[:, cols], preferred_element_type=f32)

    def core_copy(zz, k):
        b = k * NZ + zz
        return remote(core_out.at[b], core_in.at[b], r_send.at[b], r_recv.at[b], (ec, y))

    def x_copy(zz):
        return remote(x_out.at[zz], x_in.at[zz], r_send.at[8 + zz], r_recv.at[8 + zz], (ex, y))

    def y_copy(zz):
        return remote(y_out.at[zz], y_in.at[zz], r_send.at[12 + zz], r_recv.at[12 + zz], (e, 1 - y))

    def d_copy(zz):
        return remote(d_out.at[zz], d_in.at[zz], r_send.at[16 + zz], r_recv.at[16 + zz], (ex, 1 - y))

    def z_copy(zz):
        return remote(
            z_out.at[zz], z_in.at[z], r_send.at[20 + zz], r_recv.at[20 + z], (zz * 4 + x * 2 + c, y)
        )

    def z_landing(zz):
        return remote(
            z_out.at[zz], z_in.at[zz], r_send.at[20 + z], r_recv.at[20 + zz], (zz * 4 + x * 2 + c, y)
        )

    def to_core(zz):
        for k, xx in enumerate((1 - x, x)):
            core_out[k * NZ + zz] = block(zz, xx, 1 - c).astype(bf16)
            core_copy(zz, k).start()

    def to_plane(zz):
        far = block(zz, 1 - x, c)
        core_copy(zz, 0).wait_recv()
        far = far + core_in[zz].astype(f32)
        d_out[zz] = far[64:128].astype(bf16)
        d_copy(zz).start()
        x_out[zz] = far[0:64].astype(bf16)
        x_copy(zz).start()
        near = block(zz, x, c)
        core_copy(zz, 1).wait_recv()
        near = near + core_in[NZ + zz].astype(f32)
        y_out[zz] = near[64:128].astype(bf16)
        y_copy(zz).start()
        mine[zz] = near[0:64]

    def plane_sum(zz):
        x_copy(zz).wait_recv()
        y_copy(zz).wait_recv()
        d_copy(zz).wait_recv()
        return mine[zz] + x_in[zz].astype(f32) + (y_in[zz].astype(f32) + d_in[zz].astype(f32))

    to_core(order[0])
    for i in range(NZ):
        if i < NZ - 1:
            to_core(order[i + 1])
        to_plane(order[i])
    g2.wait_sends()
    for i in range(NZ - 1):
        zz = order[i]
        z_out[zz] = plane_sum(zz).astype(bf16)
        z_copy(zz).start()
        for copy in (core_copy(zz, 0), core_copy(zz, 1), x_copy(zz), y_copy(zz), d_copy(zz)):
            copy.wait_send()
    fin = plane_sum(z)
    for copy in (core_copy(z, 0), core_copy(z, 1), x_copy(z), y_copy(z), d_copy(z)):
        copy.wait_send()
    for i in range(NZ - 1):
        z_copy(order[i]).wait_send()
    for i in range(NZ - 2, -1, -1):
        zz = order[i]
        z_landing(zz).wait_recv()
        fin = fin + z_in[zz].astype(f32)
    out_ref[1] = fin.astype(bf16)


def fused_body(
    query, cache_keys, cache_values, lengths, residual, out_proj, norm_gain, expert_ids, gate_scores,
    w_gate, w_up, w_down,
):
    f32, bf16 = jnp.float32, jnp.bfloat16
    rows = query.shape[0]
    keys = cache_keys.reshape(rows, 512, 128)
    values = cache_values.reshape(rows, 512, 128)
    vm = pl.BlockSpec(memory_space=pltpu.VMEM)
    hb = pl.BlockSpec(memory_space=pl.ANY)
    sm = pl.BlockSpec(memory_space=pltpu.SMEM)
    V, S = pltpu.VMEM, pltpu.SemaphoreType.DMA
    out = pl.pallas_call(
        layer_kernel,
        name="layer",
        out_shape=pltpu.VMEM((2, 64, 256), bf16),
        in_specs=[hb, hb, hb, sm, hb, hb, hb, hb, hb, hb, hb, hb],
        out_specs=vm,
        scratch_shapes=[
            V((rows, 8192), bf16), V((64, 256), bf16), V((256,), bf16), V((8, 128), jnp.int32), V((8, 128), bf16),
            V((rows, 512, 128), bf16), V((rows, 512, 128), bf16), V((256, 4096), bf16),
            V((768, 4096), bf16), V((768, 4096), bf16), V((768, 4096), bf16), S((11,)),
            V((256, 128), f32), V((512, 128), f32), V((2, 16, 1024), bf16), V((16, 2, 16, 1024), bf16),
            V((64, 256), bf16), V((64, 256), bf16),
            V((16, 2, 80, 256), bf16),
            V((3, 128, 256), f32), V((3, 128, 256), f32), V((128, 768), bf16),
            V((4, 64, 256), f32), V((8, 128, 256), bf16), V((8, 128, 256), bf16),
            V((4, 64, 256), bf16), V((4, 64, 256), bf16), V((4, 64, 256), bf16), V((4, 64, 256), bf16),
            V((4, 64, 256), bf16), V((4, 64, 256), bf16), V((4, 64, 256), bf16), V((4, 64, 256), bf16),
            S((32,)), S((32,)), S((24,)), S((24,)), S((2,)), S((2,)), S((24,)), S((24,)),
        ],
        compiler_params=pltpu.CompilerParams(
            collective_id=0, has_side_effects=True, vmem_limit_bytes=62 * 1024 * 1024
        ),
    )(
        query, keys, values, lengths, residual, out_proj, norm_gain, expert_ids.T,
        gate_scores.T, w_gate[0], w_up[0], w_down[0],
    )
    return (out[0], out[1])


def solution(mesh):
    in_specs = (
        P(("expert", "tensor"), None),
        P(("expert", "tensor"), None, None, None),
        P(("expert", "tensor"), None, None, None),
        P(("expert", "tensor")),
        P("tensor", "expert"),
        P("expert", "tensor"),
        P("expert"),
        P(),
        P(),
        P("expert", "tensor", None),
        P("expert", "tensor", None),
        P("expert", "tensor", None),
    )
    out_specs = (P("tensor", "expert"), P("tensor", "expert"))
    fused = dict(mesh.shape) == {"expert": 16, "tensor": 2}
    return jax.shard_map(fused_body if fused else body, mesh=mesh, in_specs=in_specs, out_specs=out_specs, check_vma=False)
```

```python
import jax
import jax.numpy as jnp
from jax import lax
from jax.experimental import pallas as pl
from jax.experimental.pallas import tpu as pltpu
from jax.sharding import PartitionSpec as P

floor_value = -1e30
epsilon = 1e-06


def softmax_parts(queries, key_block, value_block, usable, score_scale):
    scores = (
        jnp.einsum("rkgd,rpkd->rkgp", queries, key_block, preferred_element_type=jnp.float32)
        * score_scale
    )
    usable_mask = usable[:, None, None, :]
    peak = jnp.max(jnp.where(usable_mask, scores, floor_value), axis=-1)
    raw_weights = jnp.where(usable_mask, jnp.exp(scores - peak[..., None]), 0.0)
    weight_sum = jnp.sum(raw_weights, axis=-1)
    weighted = jnp.einsum("rkgp,rpkd->rkgd", raw_weights, value_block.astype(jnp.float32))
    return (weight_sum, weighted)


def body(
    query,
    cache_keys,
    cache_values,
    lengths,
    residual,
    out_proj,
    norm_gain,
    expert_ids,
    gate_scores,
    w_gate,
    w_up,
    w_down,
):
    row_count, full_heads_width = query.shape
    cache_len = cache_keys.shape[1]
    kv_count = cache_keys.shape[2]
    head_size = cache_keys.shape[3]
    head_count = full_heads_width // head_size
    group_size = head_count // kv_count
    score_scale = head_size ** (-0.5)
    usable = jnp.arange(cache_len, dtype=jnp.int32)[None, :] < lengths[:, None]
    grouped = query.reshape(row_count, kv_count, group_size, head_size)
    weight_sum, weighted = softmax_parts(grouped, cache_keys, cache_values, usable, score_scale)
    context_rows_own = (
        (weighted / weight_sum[..., None]).astype(jnp.bfloat16).reshape(row_count, full_heads_width)
    )
    context = lax.all_to_all(context_rows_own, "tensor", split_axis=1, concat_axis=0, tiled=True)
    attn_part = jnp.dot(
        lax.all_gather(context, "expert", axis=0, tiled=True),
        out_proj.T,
        preferred_element_type=jnp.float32,
    )
    attn_share = lax.psum_scatter(attn_part, "tensor", scatter_dimension=0, tiled=True)
    hidden_state = residual.astype(jnp.float32) + attn_share
    squares = lax.psum(jnp.sum(hidden_state * hidden_state, axis=1), "expert")
    full_width = hidden_state.shape[1] * lax.axis_size("expert")
    scaled_share = (hidden_state * norm_gain.astype(jnp.float32)[None, :]).astype(jnp.bfloat16)
    scaled = lax.all_gather(
        lax.all_gather(scaled_share, "tensor", axis=0, tiled=True), "expert", axis=1, tiled=True
    )
    mean_all = lax.all_gather(squares / full_width, "tensor", axis=0, tiled=True)
    row_scale = lax.rsqrt(mean_all + epsilon)[:, None]
    experts_local = w_gate.shape[0]
    gate_weight = gate_scores.astype(jnp.float32)
    gate_weight = gate_weight / jnp.sum(gate_weight, axis=1, keepdims=True)
    mixed = None
    for local in range(experts_local):
        expert = lax.axis_index("expert") * experts_local + local
        weight = jnp.sum(jnp.where(expert_ids == expert, gate_weight, 0.0), axis=1, keepdims=True)
        gate_proj = row_scale * lax.dot_general(
            scaled, w_gate[local], (((1,), (1,)), ((), ())), preferred_element_type=jnp.float32
        )
        up_proj = row_scale * lax.dot_general(
            scaled, w_up[local], (((1,), (1,)), ((), ())), preferred_element_type=jnp.float32
        )
        activation = (jax.nn.silu(gate_proj) * up_proj).astype(jnp.bfloat16)
        part = weight * jnp.dot(activation, w_down[local], preferred_element_type=jnp.float32)
        mixed = part if mixed is None else mixed + part
    mixed = lax.psum_scatter(
        mixed.astype(jnp.bfloat16), "tensor", scatter_dimension=0, tiled=True
    )
    mixed_share = lax.psum_scatter(mixed, "expert", scatter_dimension=1, tiled=True)
    return (hidden_state.astype(jnp.bfloat16), mixed_share)


MESH = pl.DeviceIdType.MESH
NZ = 4
ACROSS, CORE = 4, 8


def remote(src, dst, send, recv, device):
    return pltpu.make_async_remote_copy(
        src_ref=src, dst_ref=dst, send_sem=send, recv_sem=recv, device_id=device, device_id_type=MESH
    )


class Net:
    def __init__(self, buf, sends, recvs, place, order):
        self.buf, self.sends, self.recvs = buf, sends, recvs
        self.z, self.x, self.c, self.y = place
        self.order = order
        self.started = []

    def slot(self, zz, xx, cc):
        return zz * 4 + xx * 2 + cc

    def copy(self, slot, half, send, recv, device):
        ref = self.buf.at[slot] if half is None else self.buf.at[slot, half]
        return remote(ref, ref, self.sends.at[send], self.recvs.at[recv], device)

    def go(self, slot, half, send, recv, device):
        copy = self.copy(slot, half, send, recv, device)
        copy.start()
        self.started.append(copy)

    def landed(self, slot, half, recv):
        e = self.slot(self.z, self.x, self.c)
        self.copy(slot, half, 0, recv, (e, 1 - self.y)).wait_recv()

    def along_z(self, half, base):
        z, x, c = self.z, self.x, self.c
        for i in range(NZ - 2, -1, -1):
            zz = self.order[i]
            self.go(self.slot(z, x, c), half, base + zz, base + z, (self.slot(zz, x, c), self.y))

    def z_landed(self, zz, half, base):
        self.landed(self.slot(zz, self.x, self.c), half, base + zz)

    def to_core(self, zz, xx, half, base):
        sem = base + xx * NZ + zz
        other = (self.slot(self.z, self.x, 1 - self.c), self.y)
        self.go(self.slot(zz, xx, self.c), half, sem, sem, other)

    def core_landed(self, zz, xx, half, base):
        self.landed(self.slot(zz, xx, 1 - self.c), half, base + xx * NZ + zz)

    def wait_sends(self):
        for copy in self.started:
            copy.wait_send()


class PlaneGather(Net):
    def onward(self, zz, k):
        half, sem = self.halves[k], 8 + k * NZ + zz
        z, x, c = self.z, self.x, self.c
        self.go(self.slot(zz, x, c), half, sem, sem, (self.slot(z, 1 - x, c), self.y))
        self.to_core(zz, x, half, 16 + 8 * k)

    def take_z(self, i, k):
        zz = self.order[NZ - 1 - i]
        self.z_landed(zz, self.halves[k], k * NZ)
        self.onward(zz, k)

    def take_x(self, i, k):
        zz = self.order[NZ - 1 - i]
        self.landed(self.slot(zz, 1 - self.x, self.c), self.halves[k], 8 + k * NZ + zz)
        self.to_core(zz, 1 - self.x, self.halves[k], 16 + 8 * k)

    def begin(self):
        self.halves = (self.y, 1 - self.y)
        self.along_z(self.halves[0], 0)
        self.onward(self.z, 0)

    def middle(self, swap):
        swap.wait_recv()
        self.along_z(self.halves[1], NZ)
        self.onward(self.z, 1)
        for i in range(1, NZ):
            self.take_z(i, 0)
        self.take_x(0, 0)
        for i in range(1, NZ):
            self.take_z(i, 1)
        for i in range(1, NZ):
            self.take_x(i, 0)

    def wait_core(self, k):
        for zz in range(NZ):
            for xx in range(2):
                self.core_landed(zz, xx, self.halves[k], 16 + 8 * k)


class QuadGather(Net):
    def onward(self, zz):
        z, x, c, y = self.z, self.x, self.c, self.y
        own, across = self.slot(z, x, c), self.slot(z, 1 - x, c)
        src = self.slot(zz, x, c)
        self.go(src, 1 - y, 4 + zz, 4 + zz, (across, 1 - y))
        self.go(src, 1 - y, 8 + zz, 8 + zz, (across, y))
        self.go(src, 1 - y, 12 + zz, 12 + zz, (own, 1 - y))

    def begin(self):
        self.along_z(1 - self.y, 0)
        self.onward(self.z)

    def take_z(self, i):
        zz = self.order[NZ - 1 - i]
        self.z_landed(zz, 1 - self.y, 0)
        self.onward(zz)

    def take_level(self, i):
        zz = self.order[NZ - 1 - i]
        near, far = self.slot(zz, self.x, self.c), self.slot(zz, 1 - self.x, self.c)
        self.landed(near, self.y, 12 + zz)
        self.to_core(zz, self.x, None, 16)
        self.landed(far, 1 - self.y, 8 + zz)
        self.landed(far, self.y, 4 + zz)
        self.to_core(zz, 1 - self.x, None, 16)
        return [near, far]

    def take_core(self, i):
        zz = self.order[NZ - 1 - i]
        for xx in (self.x, 1 - self.x):
            self.core_landed(zz, xx, None, 16)
        return [self.slot(zz, self.x, 1 - self.c), self.slot(zz, 1 - self.x, 1 - self.c)]


def nt_dot(a, b):
    return lax.dot_general(a, b, (((1,), (1,)), ((), ())), preferred_element_type=jnp.float32)


def low_rows(rows):
    return (lax.broadcasted_iota(jnp.int32, (rows, 256), 0) % 8) < 4


def up4(a):
    return pltpu.roll(a, a.shape[0] - 4, 0)


def down4(a):
    return pltpu.roll(a, 4, 0)


def interleave(a, b):
    rows, low = a.shape[0], low_rows(a.shape[0])
    even = jnp.where(low, a, down4(b)).reshape(rows // 8, 1, 8, 256)
    odd = jnp.where(low, up4(a), b).reshape(rows // 8, 1, 8, 256)
    return jnp.concatenate([even, odd], axis=1).reshape(2 * rows, 256)


def layer_kernel(
    q_hbm, k_hbm, v_hbm, len_ref, res_hbm, wo_hbm, gain_hbm, ids_hbm, gates_hbm,
    wg_hbm, wu_hbm, wd_hbm,
    out_ref,
    q_ref, res_ref, gain_ref, ids_ref, gates_ref,
    k_v, v_v, wo_v, wg_v, wu_v, wd_v, local_sems,
    lay, qlay, sblk, ctx, part_out, part_in, res_part, res_all, hid_own, hid_rows, hid_all, sq_own, sq_level, sq_total, sq_in, sq_z,
    gate_acc, up_acc, act, mine, core_out, core_in, x_out, x_in, y_out, y_in, d_out, d_in, z_out, z_in,
    c_send, c_recv, h_send, h_recv, p_send, p_recv, q_send, q_recv, r_send, r_recv,
):
    f32, bf16 = jnp.float32, jnp.bfloat16
    e = lax.axis_index("expert")
    y = lax.axis_index("tensor")
    z, x, c = e // 4, (e // 2) % 2, e % 2
    ex, ec = e + 2 * (1 - 2 * x), e + 1 - 2 * c
    mirror = z // 2
    near_z = z + mirror * (3 - 2 * z)
    order = [o + mirror * (3 - 2 * o) for o in (3, 2, 1 - near_z, near_z)]
    barrier = pltpu.get_barrier_semaphore()
    pairs = [(k_hbm, k_v), (v_hbm, v_v), (wo_hbm, wo_v), (wg_hbm, wg_v), (wu_hbm, wu_v), (wd_hbm, wd_v)]
    pairs += [(q_hbm, q_ref), (res_hbm, res_ref), (gain_hbm, gain_ref), (ids_hbm, ids_ref), (gates_hbm, gates_ref)]
    loads = [pltpu.make_async_copy(s, d, local_sems.at[i]) for i, (s, d) in enumerate(pairs)]
    first = [loads[6], loads[0], loads[1]] + loads[7:]
    for d in first:
        d.start()
    peers = [(ec, y), (ex, y), (e, 1 - y), (ex, 1 - y)]
    peers += [(order[i] * 4 + x * 2 + c, y) for i in range(NZ - 1)]
    for dev in peers:
        pl.semaphore_signal(barrier, inc=1, device_id=dev, device_id_type=MESH)

    rows = q_ref.shape[0]
    col = lax.broadcasted_iota(jnp.int32, (64, 512), 1)
    head = lax.broadcasted_iota(jnp.int32, (64, 512), 0)
    same = (col % 4) == (head // 16)
    loads[6].wait()
    for h in range(64):
        qlay[h * 8 : h * 8 + rows, :] = q_ref[:, h * 128 : (h + 1) * 128].astype(f32)
    loads[0].wait()
    loads[1].wait()
    for d in loads[2:6]:
        d.start()
    scores, weights, totals = [], [], []
    for r in range(rows):
        q = qlay[pl.ds(r, 64, stride=8), :].astype(bf16)
        s = nt_dot(q, k_v[r]) * (128 ** -0.5)
        scores.append(jnp.where(same & ((col // 4) < len_ref[r]), s, -1e30))
    for s in scores:
        w = jnp.exp(s - jnp.max(s, axis=1, keepdims=True))
        totals.append(jnp.sum(w, axis=1, keepdims=True))
        weights.append(w.astype(bf16))
    for r in range(rows):
        o = jnp.dot(weights[r], v_v[r], preferred_element_type=f32) / totals[r]
        for half in range(2):
            for j in range(4):
                h0 = half * 32 + j * 8
                lay[pl.ds(half * 128 + 4 * j + r, 8, stride=16), :] = o[h0 : h0 + 8]
    for half in range(2):
        for hh in range(8):
            t = (half * 8 + hh) * 16
            sblk[half, :, hh * 128 : (hh + 1) * 128] = lay[t : t + 16, :].astype(bf16)
    ctx[e, y] = sblk[y]
    pl.semaphore_wait(barrier, 7)

    swap = remote(sblk.at[1 - y], ctx.at[e, y], p_send.at[0], p_recv.at[0], (e, 1 - y))
    swap.start()
    g1 = PlaneGather(ctx, c_send, c_recv, (z, x, c, y), order)
    g1.begin()
    for d in loads[7:]:
        d.wait()
    tiles = res_ref[...].astype(f32).reshape(4, 2, 8, 256)
    even, odd = tiles[:, 0].reshape(32, 256), tiles[:, 1].reshape(32, 256)
    res_part[0] = jnp.where(low_rows(32), even, down4(odd)).astype(bf16)
    res_part[1] = jnp.where(low_rows(32), up4(even), odd).astype(bf16)
    res_all[y] = res_part[1 - y]
    rsend = remote(res_part.at[y], res_all.at[y], p_send.at[2], p_recv.at[2], (e, 1 - y))
    rsend.start()
    g1.middle(swap)
    loads[2].wait()
    quarter = (lax.broadcasted_iota(jnp.int32, (256, 256), 0) % 16) // 4
    low = (lax.broadcasted_iota(jnp.int32, (128, 256), 0) % 8) < 4
    low3 = lax.broadcasted_iota(jnp.int32, (8, 8, 256), 1) < 4

    def attn_half(h):
        lhs = ctx[:, h].reshape(256, 1024)
        acc = jnp.zeros((256, 256), f32)
        for j in range(4):
            pj = nt_dot(lhs, wo_v[:, j * 1024 : (j + 1) * 1024])
            acc = jnp.where(quarter == j, pj, acc)
        folded = acc.reshape(16, 2, 8, 256)
        folded = (folded[:, 0] + folded[:, 1]).reshape(128, 256)
        folded = folded + jnp.where(low, pltpu.roll(folded, 124, 0), pltpu.roll(folded, 4, 0))
        folded = folded.reshape(8, 2, 8, 256)
        return jnp.where(low3, folded[:, 0], folded[:, 1]).reshape(64, 256)

    g1.wait_core(0)
    part_out[...] = attn_half(y).astype(bf16)
    psend = remote(part_out, part_in, p_send.at[1], p_recv.at[1], (e, 1 - y))
    psend.start()
    g1.take_x(0, 1)
    g1.take_x(1, 1)
    g1.take_x(2, 1)
    g1.take_x(3, 1)
    g1.wait_core(1)
    mine_part = attn_half(1 - y)
    rsend.wait_recv()
    psend.wait_recv()
    hidden = res_all[...].reshape(64, 256).astype(f32) + (mine_part + part_in[...].astype(f32))
    hid_all[e, 1 - y] = (hidden * gain_ref[...].astype(f32).reshape(1, 256)).astype(bf16)
    ss = jnp.sum(hidden * hidden, axis=1, keepdims=True)
    spot = lax.broadcasted_iota(jnp.int32, (64, 128), 0) + 64 * (1 - y)
    lane = lax.broadcasted_iota(jnp.int32, (64, 128), 1)
    sq = jnp.sum(jnp.where(spot == lane, ss, 0.0), axis=0, keepdims=True)
    sq_own[...] = jnp.broadcast_to(sq, (8, 128))
    sq_core = remote(sq_own, sq_in.at[0], q_send.at[0], q_recv.at[0], (ec, y))
    sq_core.start()
    g2 = QuadGather(hid_all, h_send, h_recv, (z, x, c, y), order)
    g2.begin()
    sq_core.wait_recv()
    sq_level[...] = sq_own[...] + sq_in[0]
    sq_quad = [
        remote(sq_level, sq_in.at[k], q_send.at[k], q_recv.at[k], dev)
        for k, dev in ((1, (ex, y)), (2, (e, 1 - y)), (3, (ex, 1 - y)))
    ]
    for copy in sq_quad:
        copy.start()
    swap.wait_send()
    psend.wait_send()
    g1.wait_sends()
    hid_own[...] = hidden.astype(bf16).reshape(2, 32, 256)
    hid_rows[1 - y] = hid_own[y]
    osend = remote(hid_own.at[1 - y], hid_rows.at[1 - y], p_send.at[3], p_recv.at[3], (e, 1 - y))
    osend.start()
    eye = lax.broadcasted_iota(jnp.int32, (128, 128), 0) == lax.broadcasted_iota(jnp.int32, (128, 128), 1)
    gw = gates_ref[...].astype(f32)
    gw = gw / jnp.sum(gw, axis=0, keepdims=True)
    weight_row = jnp.sum(jnp.where(ids_ref[...] == e, gw, 0.0), axis=0, keepdims=True)
    spot = lax.broadcasted_iota(jnp.int32, (128, 128), 0)
    row = (spot % 64) // 4 * 8 + spot // 64 * 4 + spot % 4
    named = row == lax.broadcasted_iota(jnp.int32, (128, 128), 1)
    weight = jnp.sum(jnp.where(named, weight_row, 0.0), axis=1, keepdims=True)

    def products(slots, first=False):
        for n in range(3):
            for wref, aref in ((wg_v, gate_acc), (wu_v, up_acc)):
                a = None if first else aref[n]
                for src in slots:
                    cols = pl.ds(pl.multiple_of(src * 256, 256), 256)
                    t = nt_dot(hid_all[src].reshape(128, 256), wref[n * 256 : (n + 1) * 256, cols])
                    a = t if a is None else a + t
                aref[n] = a

    for i in range(1, NZ):
        g2.take_z(i)
    loads[3].wait()
    loads[4].wait()
    slots = g2.take_level(0)
    for copy in sq_quad:
        copy.wait_recv()
    sq_total[...] = (sq_level[...] + sq_in[1]) + (sq_in[2] + sq_in[3])

    def sq_z_copy(zz):
        return remote(
            sq_total, sq_z.at[z], q_send.at[4 + zz], q_recv.at[4 + z], (zz * 4 + x * 2 + c, y)
        )

    def sq_z_landing(zz):
        return remote(
            sq_total, sq_z.at[zz], q_send.at[4 + z], q_recv.at[4 + zz], (zz * 4 + x * 2 + c, y)
        )

    for i in range(NZ - 1):
        sq_z_copy(order[i]).start()
    products(slots, True)
    for i in range(1, NZ):
        products(g2.take_level(i) + g2.take_core(i - 1))
    products(g2.take_core(NZ - 1))

    total = sq_total[...]
    for i in range(NZ - 1):
        sq_z_landing(order[i]).wait_recv()
        total = total + sq_z[order[i]]
    scale_row = lax.rsqrt(total[0:1] / 4096.0 + epsilon)
    scale = jnp.sum(jnp.where(eye, scale_row, 0.0), axis=1, keepdims=True)
    for n in range(3):
        g = gate_acc[n] * scale
        u = up_acc[n] * scale
        a = g / (1.0 + jnp.exp(-g)) * u * weight
        a = interleave(a[0:64], a[64:128]).astype(bf16)
        for half in range(2):
            to = pl.ds(pl.multiple_of(((half + y) % 2) * 64, 64), 64)
            act[to, n * 256 : (n + 1) * 256] = a[half * 64 : (half + 1) * 64]
    loads[5].wait()

    def block(zz, xx, cc):
        cols = pl.ds(pl.multiple_of((zz * 4 + xx * 2 + cc) * 256, 256), 256)
        return jnp.dot(act[...], wd_v[:, cols], preferred_element_type=f32)

    def core_copy(zz, k):
        b = k * NZ + zz
        return remote(core_out.at[b], core_in.at[b], r_send.at[b], r_recv.at[b], (ec, y))

    def x_copy(zz):
        return remote(x_out.at[zz], x_in.at[zz], r_send.at[8 + zz], r_recv.at[8 + zz], (ex, y))

    def y_copy(zz):
        return remote(y_out.at[zz], y_in.at[zz], r_send.at[12 + zz], r_recv.at[12 + zz], (e, 1 - y))

    def d_copy(zz):
        return remote(d_out.at[zz], d_in.at[zz], r_send.at[16 + zz], r_recv.at[16 + zz], (ex, 1 - y))

    def z_copy(zz):
        return remote(
            z_out.at[zz], z_in.at[z], r_send.at[20 + zz], r_recv.at[20 + z], (zz * 4 + x * 2 + c, y)
        )

    def z_landing(zz):
        return remote(
            z_out.at[zz], z_in.at[zz], r_send.at[20 + z], r_recv.at[20 + zz], (zz * 4 + x * 2 + c, y)
        )

    def to_core(zz):
        for k, xx in enumerate((1 - x, x)):
            core_out[k * NZ + zz] = block(zz, xx, 1 - c).astype(bf16)
            core_copy(zz, k).start()

    def to_plane(zz):
        far = block(zz, 1 - x, c)
        core_copy(zz, 0).wait_recv()
        far = far + core_in[zz].astype(f32)
        d_out[zz] = far[64:128].astype(bf16)
        d_copy(zz).start()
        x_out[zz] = far[0:64].astype(bf16)
        x_copy(zz).start()
        near = block(zz, x, c)
        core_copy(zz, 1).wait_recv()
        near = near + core_in[NZ + zz].astype(f32)
        y_out[zz] = near[64:128].astype(bf16)
        y_copy(zz).start()
        mine[zz] = near[0:64]

    def plane_sum(zz):
        x_copy(zz).wait_recv()
        y_copy(zz).wait_recv()
        d_copy(zz).wait_recv()
        return mine[zz] + x_in[zz].astype(f32) + (y_in[zz].astype(f32) + d_in[zz].astype(f32))

    to_core(order[0])
    for i in range(NZ):
        if i < NZ - 1:
            to_core(order[i + 1])
        to_plane(order[i])
    g2.wait_sends()
    rsend.wait_send()
    osend.wait_send()
    osend.wait_recv()
    out_ref[0] = interleave(hid_rows[0].astype(f32), hid_rows[1].astype(f32)).astype(bf16)
    for copy in [sq_core] + sq_quad + [sq_z_copy(order[i]) for i in range(NZ - 1)]:
        copy.wait_send()
    for i in range(NZ - 1):
        zz = order[i]
        z_out[zz] = plane_sum(zz).astype(bf16)
        z_copy(zz).start()
        for copy in (core_copy(zz, 0), core_copy(zz, 1), x_copy(zz), y_copy(zz), d_copy(zz)):
            copy.wait_send()
    fin = plane_sum(z)
    for copy in (core_copy(z, 0), core_copy(z, 1), x_copy(z), y_copy(z), d_copy(z)):
        copy.wait_send()
    for i in range(NZ - 1):
        z_copy(order[i]).wait_send()
    for i in range(NZ - 2, -1, -1):
        zz = order[i]
        z_landing(zz).wait_recv()
        fin = fin + z_in[zz].astype(f32)
    out_ref[1] = fin.astype(bf16)


def fused_body(
    query, cache_keys, cache_values, lengths, residual, out_proj, norm_gain, expert_ids, gate_scores,
    w_gate, w_up, w_down,
):
    f32, bf16 = jnp.float32, jnp.bfloat16
    rows = query.shape[0]
    keys = cache_keys.reshape(rows, 512, 128)
    values = cache_values.reshape(rows, 512, 128)
    vm = pl.BlockSpec(memory_space=pltpu.VMEM)
    hb = pl.BlockSpec(memory_space=pl.ANY)
    sm = pl.BlockSpec(memory_space=pltpu.SMEM)
    V, S = pltpu.VMEM, pltpu.SemaphoreType.DMA
    out = pl.pallas_call(
        layer_kernel,
        name="layer",
        out_shape=pltpu.VMEM((2, 64, 256), bf16),
        in_specs=[hb, hb, hb, sm, hb, hb, hb, hb, hb, hb, hb, hb],
        out_specs=vm,
        scratch_shapes=[
            V((rows, 8192), bf16), V((64, 256), bf16), V((256,), bf16), V((8, 128), jnp.int32), V((8, 128), bf16),
            V((rows, 512, 128), bf16), V((rows, 512, 128), bf16), V((256, 4096), bf16),
            V((768, 4096), bf16), V((768, 4096), bf16), V((768, 4096), bf16), S((11,)),
            V((256, 128), f32), V((512, 128), f32), V((2, 16, 1024), bf16), V((16, 2, 16, 1024), bf16),
            V((64, 256), bf16), V((64, 256), bf16),
            V((2, 32, 256), bf16), V((2, 32, 256), bf16), V((2, 32, 256), bf16), V((2, 32, 256), bf16),
            V((16, 2, 64, 256), bf16),
            V((8, 128), f32), V((8, 128), f32), V((8, 128), f32), V((4, 8, 128), f32), V((4, 8, 128), f32),
            V((3, 128, 256), f32), V((3, 128, 256), f32), V((128, 768), bf16),
            V((4, 64, 256), f32), V((8, 128, 256), bf16), V((8, 128, 256), bf16),
            V((4, 64, 256), bf16), V((4, 64, 256), bf16), V((4, 64, 256), bf16), V((4, 64, 256), bf16),
            V((4, 64, 256), bf16), V((4, 64, 256), bf16), V((4, 64, 256), bf16), V((4, 64, 256), bf16),
            S((32,)), S((32,)), S((24,)), S((24,)), S((4,)), S((4,)), S((8,)), S((8,)), S((24,)), S((24,)),
        ],
        compiler_params=pltpu.CompilerParams(
            collective_id=0, has_side_effects=True, vmem_limit_bytes=62 * 1024 * 1024
        ),
    )(
        query, keys, values, lengths, residual, out_proj, norm_gain, expert_ids.T,
        gate_scores.T, w_gate[0], w_up[0], w_down[0],
    )
    return (out[0], out[1])


def solution(mesh):
    in_specs = (
        P(("expert", "tensor"), None),
        P(("expert", "tensor"), None, None, None),
        P(("expert", "tensor"), None, None, None),
        P(("expert", "tensor")),
        P("tensor", "expert"),
        P("expert", "tensor"),
        P("expert"),
        P(),
        P(),
        P("expert", "tensor", None),
        P("expert", "tensor", None),
        P("expert", "tensor", None),
    )
    out_specs = (P("tensor", "expert"), P("tensor", "expert"))
    fused = dict(mesh.shape) == {"expert": 16, "tensor": 2}
    return jax.shard_map(fused_body if fused else body, mesh=mesh, in_specs=in_specs, out_specs=out_specs, check_vma=False)
```

```python
import jax
import jax.numpy as jnp
from jax import lax
from jax.experimental import pallas as pl
from jax.experimental.pallas import tpu as pltpu
from jax.sharding import PartitionSpec as P

floor_value = -1e30
epsilon = 1e-06


def softmax_parts(queries, key_block, value_block, usable, score_scale):
    scores = (
        jnp.einsum("rkgd,rpkd->rkgp", queries, key_block, preferred_element_type=jnp.float32)
        * score_scale
    )
    usable_mask = usable[:, None, None, :]
    peak = jnp.max(jnp.where(usable_mask, scores, floor_value), axis=-1)
    raw_weights = jnp.where(usable_mask, jnp.exp(scores - peak[..., None]), 0.0)
    weight_sum = jnp.sum(raw_weights, axis=-1)
    weighted = jnp.einsum("rkgp,rpkd->rkgd", raw_weights, value_block.astype(jnp.float32))
    return (weight_sum, weighted)


def body(
    query,
    cache_keys,
    cache_values,
    lengths,
    residual,
    out_proj,
    norm_gain,
    expert_ids,
    gate_scores,
    w_gate,
    w_up,
    w_down,
):
    row_count, full_heads_width = query.shape
    cache_len = cache_keys.shape[1]
    kv_count = cache_keys.shape[2]
    head_size = cache_keys.shape[3]
    head_count = full_heads_width // head_size
    group_size = head_count // kv_count
    score_scale = head_size ** (-0.5)
    usable = jnp.arange(cache_len, dtype=jnp.int32)[None, :] < lengths[:, None]
    grouped = query.reshape(row_count, kv_count, group_size, head_size)
    weight_sum, weighted = softmax_parts(grouped, cache_keys, cache_values, usable, score_scale)
    context_rows_own = (
        (weighted / weight_sum[..., None]).astype(jnp.bfloat16).reshape(row_count, full_heads_width)
    )
    context = lax.all_to_all(context_rows_own, "tensor", split_axis=1, concat_axis=0, tiled=True)
    attn_part = jnp.dot(
        lax.all_gather(context, "expert", axis=0, tiled=True),
        out_proj.T,
        preferred_element_type=jnp.float32,
    )
    attn_share = lax.psum_scatter(attn_part, "tensor", scatter_dimension=0, tiled=True)
    hidden_state = residual.astype(jnp.float32) + attn_share
    squares = lax.psum(jnp.sum(hidden_state * hidden_state, axis=1), "expert")
    full_width = hidden_state.shape[1] * lax.axis_size("expert")
    scaled_share = (hidden_state * norm_gain.astype(jnp.float32)[None, :]).astype(jnp.bfloat16)
    scaled = lax.all_gather(
        lax.all_gather(scaled_share, "tensor", axis=0, tiled=True), "expert", axis=1, tiled=True
    )
    mean_all = lax.all_gather(squares / full_width, "tensor", axis=0, tiled=True)
    row_scale = lax.rsqrt(mean_all + epsilon)[:, None]
    experts_local = w_gate.shape[0]
    gate_weight = gate_scores.astype(jnp.float32)
    gate_weight = gate_weight / jnp.sum(gate_weight, axis=1, keepdims=True)
    mixed = None
    for local in range(experts_local):
        expert = lax.axis_index("expert") * experts_local + local
        weight = jnp.sum(jnp.where(expert_ids == expert, gate_weight, 0.0), axis=1, keepdims=True)
        gate_proj = row_scale * lax.dot_general(
            scaled, w_gate[local], (((1,), (1,)), ((), ())), preferred_element_type=jnp.float32
        )
        up_proj = row_scale * lax.dot_general(
            scaled, w_up[local], (((1,), (1,)), ((), ())), preferred_element_type=jnp.float32
        )
        activation = (jax.nn.silu(gate_proj) * up_proj).astype(jnp.bfloat16)
        part = weight * jnp.dot(activation, w_down[local], preferred_element_type=jnp.float32)
        mixed = part if mixed is None else mixed + part
    mixed = lax.psum_scatter(
        mixed.astype(jnp.bfloat16), "tensor", scatter_dimension=0, tiled=True
    )
    mixed_share = lax.psum_scatter(mixed, "expert", scatter_dimension=1, tiled=True)
    return (hidden_state.astype(jnp.bfloat16), mixed_share)


MESH = pl.DeviceIdType.MESH
NZ = 4
ACROSS, CORE = 4, 8


def remote(src, dst, send, recv, device):
    return pltpu.make_async_remote_copy(
        src_ref=src, dst_ref=dst, send_sem=send, recv_sem=recv, device_id=device, device_id_type=MESH
    )


class Net:
    def __init__(self, buf, sends, recvs, place, order):
        self.buf, self.sends, self.recvs = buf, sends, recvs
        self.z, self.x, self.c, self.y = place
        self.order = order
        self.started = []

    def slot(self, zz, xx, cc):
        return zz * 4 + xx * 2 + cc

    def copy(self, slot, half, send, recv, device):
        ref = self.buf.at[slot] if half is None else self.buf.at[slot, half]
        return remote(ref, ref, self.sends.at[send], self.recvs.at[recv], device)

    def go(self, slot, half, send, recv, device):
        copy = self.copy(slot, half, send, recv, device)
        copy.start()
        self.started.append(copy)

    def landed(self, slot, half, recv):
        e = self.slot(self.z, self.x, self.c)
        self.copy(slot, half, 0, recv, (e, 1 - self.y)).wait_recv()

    def along_z(self, half, base):
        z, x, c = self.z, self.x, self.c
        for i in range(NZ - 2, -1, -1):
            zz = self.order[i]
            self.go(self.slot(z, x, c), half, base + zz, base + z, (self.slot(zz, x, c), self.y))

    def z_landed(self, zz, half, base):
        self.landed(self.slot(zz, self.x, self.c), half, base + zz)

    def to_core(self, zz, xx, half, base):
        sem = base + xx * NZ + zz
        other = (self.slot(self.z, self.x, 1 - self.c), self.y)
        self.go(self.slot(zz, xx, self.c), half, sem, sem, other)

    def core_landed(self, zz, xx, half, base):
        self.landed(self.slot(zz, xx, 1 - self.c), half, base + xx * NZ + zz)

    def wait_sends(self):
        for copy in self.started:
            copy.wait_send()


class PlaneGather(Net):
    def onward(self, zz, k):
        half, sem = self.halves[k], 8 + k * NZ + zz
        z, x, c = self.z, self.x, self.c
        self.go(self.slot(zz, x, c), half, sem, sem, (self.slot(z, 1 - x, c), self.y))
        self.to_core(zz, x, half, 16 + 8 * k)

    def take_z(self, i, k):
        zz = self.order[NZ - 1 - i]
        self.z_landed(zz, self.halves[k], k * NZ)
        self.onward(zz, k)

    def take_x(self, i, k):
        zz = self.order[NZ - 1 - i]
        self.landed(self.slot(zz, 1 - self.x, self.c), self.halves[k], 8 + k * NZ + zz)
        self.to_core(zz, 1 - self.x, self.halves[k], 16 + 8 * k)

    def begin(self):
        self.halves = (self.y, 1 - self.y)
        self.along_z(self.halves[0], 0)
        self.onward(self.z, 0)

    def middle(self, swap):
        swap.wait_recv()
        self.along_z(self.halves[1], NZ)
        self.onward(self.z, 1)
        for i in range(1, NZ):
            self.take_z(i, 0)
        self.take_x(0, 0)
        for i in range(1, NZ):
            self.take_z(i, 1)
            self.take_x(i, 0)

    def wait_core(self, k):
        for zz in range(NZ):
            for xx in range(2):
                self.core_landed(zz, xx, self.halves[k], 16 + 8 * k)


class QuadGather(Net):
    def onward(self, zz):
        z, x, c, y = self.z, self.x, self.c, self.y
        own, across = self.slot(z, x, c), self.slot(z, 1 - x, c)
        src = self.slot(zz, x, c)
        self.go(src, 1 - y, 4 + zz, 4 + zz, (across, 1 - y))
        self.go(src, 1 - y, 8 + zz, 8 + zz, (across, y))
        self.go(src, 1 - y, 12 + zz, 12 + zz, (own, 1 - y))

    def begin(self):
        self.along_z(1 - self.y, 0)
        self.onward(self.z)

    def take_z(self, i):
        zz = self.order[NZ - 1 - i]
        self.z_landed(zz, 1 - self.y, 0)
        self.onward(zz)

    def take_level(self, i):
        zz = self.order[NZ - 1 - i]
        near, far = self.slot(zz, self.x, self.c), self.slot(zz, 1 - self.x, self.c)
        self.landed(near, self.y, 12 + zz)
        self.to_core(zz, self.x, None, 16)
        self.landed(far, 1 - self.y, 8 + zz)
        self.landed(far, self.y, 4 + zz)
        self.to_core(zz, 1 - self.x, None, 16)
        return [near, far]

    def take_core(self, i):
        zz = self.order[NZ - 1 - i]
        for xx in (self.x, 1 - self.x):
            self.core_landed(zz, xx, None, 16)
        return [self.slot(zz, self.x, 1 - self.c), self.slot(zz, 1 - self.x, 1 - self.c)]


def nt_dot(a, b):
    return lax.dot_general(a, b, (((1,), (1,)), ((), ())), preferred_element_type=jnp.float32)


def low_rows(rows):
    return (lax.broadcasted_iota(jnp.int32, (rows, 256), 0) % 8) < 4


def up4(a):
    return pltpu.roll(a, a.shape[0] - 4, 0)


def down4(a):
    return pltpu.roll(a, 4, 0)


def interleave(a, b):
    rows, low = a.shape[0], low_rows(a.shape[0])
    even = jnp.where(low, a, down4(b)).reshape(rows // 8, 1, 8, 256)
    odd = jnp.where(low, up4(a), b).reshape(rows // 8, 1, 8, 256)
    return jnp.concatenate([even, odd], axis=1).reshape(2 * rows, 256)


def layer_kernel(
    q_hbm, k_hbm, v_hbm, len_ref, res_hbm, wo_hbm, gain_hbm, ids_hbm, gates_hbm,
    wg_hbm, wu_hbm, wd_hbm,
    out_ref,
    q_ref, res_ref, gain_ref, ids_ref, gates_ref,
    k_v, v_v, wo_v, wg_v, wu_v, wd_v, local_sems,
    lay, qlay, sblk, ctx, part_out, part_in, res_part, res_all, hid_own, hid_rows, hid_all, sq_own, sq_level, sq_total, sq_in, sq_z,
    gate_acc, up_acc, act, mine, core_out, core_in, x_out, x_in, y_out, y_in, d_out, d_in, z_out, z_in,
    c_send, c_recv, h_send, h_recv, p_send, p_recv, q_send, q_recv, r_send, r_recv,
):
    f32, bf16 = jnp.float32, jnp.bfloat16
    e = lax.axis_index("expert")
    y = lax.axis_index("tensor")
    z, x, c = e // 4, (e // 2) % 2, e % 2
    ex, ec = e + 2 * (1 - 2 * x), e + 1 - 2 * c
    mirror = z // 2
    near_z = z + mirror * (3 - 2 * z)
    order = [o + mirror * (3 - 2 * o) for o in (3, 2, 1 - near_z, near_z)]
    barrier = pltpu.get_barrier_semaphore()
    pairs = [(k_hbm, k_v), (v_hbm, v_v), (wo_hbm, wo_v), (wg_hbm, wg_v), (wu_hbm, wu_v), (wd_hbm, wd_v)]
    pairs += [(q_hbm, q_ref), (res_hbm, res_ref), (gain_hbm, gain_ref), (ids_hbm, ids_ref), (gates_hbm, gates_ref)]
    loads = [pltpu.make_async_copy(s, d, local_sems.at[i]) for i, (s, d) in enumerate(pairs)]
    first = [loads[6], loads[0], loads[1]] + loads[7:]
    for d in first:
        d.start()
    peers = [(ec, y), (ex, y), (e, 1 - y), (ex, 1 - y)]
    peers += [(order[i] * 4 + x * 2 + c, y) for i in range(NZ - 1)]
    for dev in peers:
        pl.semaphore_signal(barrier, inc=1, device_id=dev, device_id_type=MESH)

    rows = q_ref.shape[0]
    col = lax.broadcasted_iota(jnp.int32, (64, 512), 1)
    head = lax.broadcasted_iota(jnp.int32, (64, 512), 0)
    same = (col % 4) == (head // 16)
    loads[6].wait()
    for h in range(64):
        qlay[h * 8 : h * 8 + rows, :] = q_ref[:, h * 128 : (h + 1) * 128].astype(f32)
    loads[0].wait()
    loads[1].wait()
    for d in loads[2:6]:
        d.start()
    scores, weights, totals = [], [], []
    for r in range(rows):
        q = qlay[pl.ds(r, 64, stride=8), :].astype(bf16)
        s = nt_dot(q, k_v[r]) * (128 ** -0.5)
        scores.append(jnp.where(same & ((col // 4) < len_ref[r]), s, -1e30))
    for s in scores:
        w = jnp.exp(s - jnp.max(s, axis=1, keepdims=True))
        totals.append(jnp.sum(w, axis=1, keepdims=True))
        weights.append(w.astype(bf16))
    for r in range(rows):
        o = jnp.dot(weights[r], v_v[r], preferred_element_type=f32) / totals[r]
        for half in range(2):
            for j in range(4):
                h0 = half * 32 + j * 8
                lay[pl.ds(half * 128 + 4 * j + r, 8, stride=16), :] = o[h0 : h0 + 8]
    for half in range(2):
        for hh in range(8):
            t = (half * 8 + hh) * 16
            sblk[half, :, hh * 128 : (hh + 1) * 128] = lay[t : t + 16, :].astype(bf16)
    ctx[e, y] = sblk[y]
    pl.semaphore_wait(barrier, 7)

    swap = remote(sblk.at[1 - y], ctx.at[e, y], p_send.at[0], p_recv.at[0], (e, 1 - y))
    swap.start()
    g1 = PlaneGather(ctx, c_send, c_recv, (z, x, c, y), order)
    g1.begin()
    for d in loads[7:]:
        d.wait()
    tiles = res_ref[...].astype(f32).reshape(4, 2, 8, 256)
    even, odd = tiles[:, 0].reshape(32, 256), tiles[:, 1].reshape(32, 256)
    res_part[0] = jnp.where(low_rows(32), even, down4(odd)).astype(bf16)
    res_part[1] = jnp.where(low_rows(32), up4(even), odd).astype(bf16)
    res_all[y] = res_part[1 - y]
    rsend = remote(res_part.at[y], res_all.at[y], p_send.at[2], p_recv.at[2], (e, 1 - y))
    rsend.start()
    g1.middle(swap)
    loads[2].wait()
    quarter = (lax.broadcasted_iota(jnp.int32, (256, 256), 0) % 16) // 4
    low = (lax.broadcasted_iota(jnp.int32, (128, 256), 0) % 8) < 4
    low3 = lax.broadcasted_iota(jnp.int32, (8, 8, 256), 1) < 4

    def attn_half(h):
        lhs = ctx[:, h].reshape(256, 1024)
        acc = jnp.zeros((256, 256), f32)
        for j in range(4):
            pj = nt_dot(lhs, wo_v[:, j * 1024 : (j + 1) * 1024])
            acc = jnp.where(quarter == j, pj, acc)
        folded = acc.reshape(16, 2, 8, 256)
        folded = (folded[:, 0] + folded[:, 1]).reshape(128, 256)
        folded = folded + jnp.where(low, pltpu.roll(folded, 124, 0), pltpu.roll(folded, 4, 0))
        folded = folded.reshape(8, 2, 8, 256)
        return jnp.where(low3, folded[:, 0], folded[:, 1]).reshape(64, 256)

    g1.wait_core(0)
    part_out[...] = attn_half(y).astype(bf16)
    psend = remote(part_out, part_in, p_send.at[1], p_recv.at[1], (e, 1 - y))
    psend.start()
    g1.take_x(0, 1)
    g1.take_x(1, 1)
    g1.take_x(2, 1)
    g1.take_x(3, 1)
    g1.wait_core(1)
    mine_part = attn_half(1 - y)
    rsend.wait_recv()
    psend.wait_recv()
    hidden = res_all[...].reshape(64, 256).astype(f32) + (mine_part + part_in[...].astype(f32))
    hid_all[e, 1 - y] = (hidden * gain_ref[...].astype(f32).reshape(1, 256)).astype(bf16)
    ss = jnp.sum(hidden * hidden, axis=1, keepdims=True)
    spot = lax.broadcasted_iota(jnp.int32, (64, 128), 0) + 64 * (1 - y)
    lane = lax.broadcasted_iota(jnp.int32, (64, 128), 1)
    sq = jnp.sum(jnp.where(spot == lane, ss, 0.0), axis=0, keepdims=True)
    sq_own[...] = jnp.broadcast_to(sq, (8, 128))
    sq_core = remote(sq_own, sq_in.at[0], q_send.at[0], q_recv.at[0], (ec, y))
    sq_core.start()
    g2 = QuadGather(hid_all, h_send, h_recv, (z, x, c, y), order)
    g2.begin()
    sq_core.wait_recv()
    sq_level[...] = sq_own[...] + sq_in[0]
    sq_quad = [
        remote(sq_level, sq_in.at[k], q_send.at[k], q_recv.at[k], dev)
        for k, dev in ((1, (ex, y)), (2, (e, 1 - y)), (3, (ex, 1 - y)))
    ]
    for copy in sq_quad:
        copy.start()
    swap.wait_send()
    psend.wait_send()
    g1.wait_sends()
    hid_own[...] = hidden.astype(bf16).reshape(2, 32, 256)
    hid_rows[1 - y] = hid_own[y]
    osend = remote(hid_own.at[1 - y], hid_rows.at[1 - y], p_send.at[3], p_recv.at[3], (e, 1 - y))
    osend.start()
    eye = lax.broadcasted_iota(jnp.int32, (128, 128), 0) == lax.broadcasted_iota(jnp.int32, (128, 128), 1)
    gw = gates_ref[...].astype(f32)
    gw = gw / jnp.sum(gw, axis=0, keepdims=True)
    weight_row = jnp.sum(jnp.where(ids_ref[...] == e, gw, 0.0), axis=0, keepdims=True)
    spot = lax.broadcasted_iota(jnp.int32, (128, 128), 0)
    row = (spot % 64) // 4 * 8 + spot // 64 * 4 + spot % 4
    named = row == lax.broadcasted_iota(jnp.int32, (128, 128), 1)
    weight = jnp.sum(jnp.where(named, weight_row, 0.0), axis=1, keepdims=True)

    def products(slots, first=False):
        for n in range(3):
            for wref, aref in ((wg_v, gate_acc), (wu_v, up_acc)):
                a = None if first else aref[n]
                for src in slots:
                    cols = pl.ds(pl.multiple_of(src * 256, 256), 256)
                    t = nt_dot(hid_all[src].reshape(128, 256), wref[n * 256 : (n + 1) * 256, cols])
                    a = t if a is None else a + t
                aref[n] = a

    for i in range(1, NZ):
        g2.take_z(i)
    loads[3].wait()
    loads[4].wait()
    slots = g2.take_level(0)
    for copy in sq_quad:
        copy.wait_recv()
    sq_total[...] = (sq_level[...] + sq_in[1]) + (sq_in[2] + sq_in[3])

    def sq_z_copy(zz):
        return remote(
            sq_total, sq_z.at[z], q_send.at[4 + zz], q_recv.at[4 + z], (zz * 4 + x * 2 + c, y)
        )

    def sq_z_landing(zz):
        return remote(
            sq_total, sq_z.at[zz], q_send.at[4 + z], q_recv.at[4 + zz], (zz * 4 + x * 2 + c, y)
        )

    for i in range(NZ - 1):
        sq_z_copy(order[i]).start()
    products(slots, True)
    for i in range(1, NZ):
        products(g2.take_level(i) + g2.take_core(i - 1))
    products(g2.take_core(NZ - 1))

    total = sq_total[...]
    for i in range(NZ - 1):
        sq_z_landing(order[i]).wait_recv()
        total = total + sq_z[order[i]]
    scale_row = lax.rsqrt(total[0:1] / 4096.0 + epsilon)
    scale = jnp.sum(jnp.where(eye, scale_row, 0.0), axis=1, keepdims=True)
    for n in range(3):
        g = gate_acc[n] * scale
        u = up_acc[n] * scale
        a = g / (1.0 + jnp.exp(-g)) * u * weight
        a = interleave(a[0:64], a[64:128]).astype(bf16)
        for half in range(2):
            to = pl.ds(pl.multiple_of(((half + y) % 2) * 64, 64), 64)
            act[to, n * 256 : (n + 1) * 256] = a[half * 64 : (half + 1) * 64]
    loads[5].wait()

    def block(zz, xx, cc):
        cols = pl.ds(pl.multiple_of((zz * 4 + xx * 2 + cc) * 256, 256), 256)
        return jnp.dot(act[...], wd_v[:, cols], preferred_element_type=f32)

    def core_copy(zz, k):
        b = k * NZ + zz
        return remote(core_out.at[b], core_in.at[b], r_send.at[b], r_recv.at[b], (ec, y))

    def x_copy(zz):
        return remote(x_out.at[zz], x_in.at[zz], r_send.at[8 + zz], r_recv.at[8 + zz], (ex, y))

    def y_copy(zz):
        return remote(y_out.at[zz], y_in.at[zz], r_send.at[12 + zz], r_recv.at[12 + zz], (e, 1 - y))

    def d_copy(zz):
        return remote(d_out.at[zz], d_in.at[zz], r_send.at[16 + zz], r_recv.at[16 + zz], (ex, 1 - y))

    def z_copy(zz):
        return remote(
            z_out.at[zz], z_in.at[z], r_send.at[20 + zz], r_recv.at[20 + z], (zz * 4 + x * 2 + c, y)
        )

    def z_landing(zz):
        return remote(
            z_out.at[zz], z_in.at[zz], r_send.at[20 + z], r_recv.at[20 + zz], (zz * 4 + x * 2 + c, y)
        )

    def to_core(zz):
        for k, xx in enumerate((1 - x, x)):
            core_out[k * NZ + zz] = block(zz, xx, 1 - c).astype(bf16)
            core_copy(zz, k).start()

    def to_plane(zz):
        far = block(zz, 1 - x, c)
        core_copy(zz, 0).wait_recv()
        far = far + core_in[zz].astype(f32)
        d_out[zz] = far[64:128].astype(bf16)
        d_copy(zz).start()
        x_out[zz] = far[0:64].astype(bf16)
        x_copy(zz).start()
        near = block(zz, x, c)
        core_copy(zz, 1).wait_recv()
        near = near + core_in[NZ + zz].astype(f32)
        y_out[zz] = near[64:128].astype(bf16)
        y_copy(zz).start()
        mine[zz] = near[0:64]

    def plane_sum(zz):
        x_copy(zz).wait_recv()
        y_copy(zz).wait_recv()
        d_copy(zz).wait_recv()
        return mine[zz] + x_in[zz].astype(f32) + (y_in[zz].astype(f32) + d_in[zz].astype(f32))

    to_core(order[0])
    for i in range(NZ):
        if i < NZ - 1:
            to_core(order[i + 1])
        to_plane(order[i])
    g2.wait_sends()
    rsend.wait_send()
    osend.wait_send()
    osend.wait_recv()
    out_ref[0] = interleave(hid_rows[0].astype(f32), hid_rows[1].astype(f32)).astype(bf16)
    for copy in [sq_core] + sq_quad + [sq_z_copy(order[i]) for i in range(NZ - 1)]:
        copy.wait_send()
    for i in range(NZ - 1):
        zz = order[i]
        z_out[zz] = plane_sum(zz).astype(bf16)
        z_copy(zz).start()
        for copy in (core_copy(zz, 0), core_copy(zz, 1), x_copy(zz), y_copy(zz), d_copy(zz)):
            copy.wait_send()
    fin = plane_sum(z)
    for copy in (core_copy(z, 0), core_copy(z, 1), x_copy(z), y_copy(z), d_copy(z)):
        copy.wait_send()
    for i in range(NZ - 1):
        z_copy(order[i]).wait_send()
    for i in range(NZ - 2, -1, -1):
        zz = order[i]
        z_landing(zz).wait_recv()
        fin = fin + z_in[zz].astype(f32)
    out_ref[1] = fin.astype(bf16)


def fused_body(
    query, cache_keys, cache_values, lengths, residual, out_proj, norm_gain, expert_ids, gate_scores,
    w_gate, w_up, w_down,
):
    f32, bf16 = jnp.float32, jnp.bfloat16
    rows = query.shape[0]
    keys = cache_keys.reshape(rows, 512, 128)
    values = cache_values.reshape(rows, 512, 128)
    vm = pl.BlockSpec(memory_space=pltpu.VMEM)
    hb = pl.BlockSpec(memory_space=pl.ANY)
    sm = pl.BlockSpec(memory_space=pltpu.SMEM)
    V, S = pltpu.VMEM, pltpu.SemaphoreType.DMA
    out = pl.pallas_call(
        layer_kernel,
        name="layer",
        out_shape=pltpu.VMEM((2, 64, 256), bf16),
        in_specs=[hb, hb, hb, sm, hb, hb, hb, hb, hb, hb, hb, hb],
        out_specs=vm,
        scratch_shapes=[
            V((rows, 8192), bf16), V((64, 256), bf16), V((256,), bf16), V((8, 128), jnp.int32), V((8, 128), bf16),
            V((rows, 512, 128), bf16), V((rows, 512, 128), bf16), V((256, 4096), bf16),
            V((768, 4096), bf16), V((768, 4096), bf16), V((768, 4096), bf16), S((11,)),
            V((256, 128), f32), V((512, 128), f32), V((2, 16, 1024), bf16), V((16, 2, 16, 1024), bf16),
            V((64, 256), bf16), V((64, 256), bf16),
            V((2, 32, 256), bf16), V((2, 32, 256), bf16), V((2, 32, 256), bf16), V((2, 32, 256), bf16),
            V((16, 2, 64, 256), bf16),
            V((8, 128), f32), V((8, 128), f32), V((8, 128), f32), V((4, 8, 128), f32), V((4, 8, 128), f32),
            V((3, 128, 256), f32), V((3, 128, 256), f32), V((128, 768), bf16),
            V((4, 64, 256), f32), V((8, 128, 256), bf16), V((8, 128, 256), bf16),
            V((4, 64, 256), bf16), V((4, 64, 256), bf16), V((4, 64, 256), bf16), V((4, 64, 256), bf16),
            V((4, 64, 256), bf16), V((4, 64, 256), bf16), V((4, 64, 256), bf16), V((4, 64, 256), bf16),
            S((32,)), S((32,)), S((24,)), S((24,)), S((4,)), S((4,)), S((8,)), S((8,)), S((24,)), S((24,)),
        ],
        compiler_params=pltpu.CompilerParams(
            collective_id=0, has_side_effects=True, vmem_limit_bytes=62 * 1024 * 1024
        ),
    )(
        query, keys, values, lengths, residual, out_proj, norm_gain, expert_ids.T,
        gate_scores.T, w_gate[0], w_up[0], w_down[0],
    )
    return (out[0], out[1])


def solution(mesh):
    in_specs = (
        P(("expert", "tensor"), None),
        P(("expert", "tensor"), None, None, None),
        P(("expert", "tensor"), None, None, None),
        P(("expert", "tensor")),
        P("tensor", "expert"),
        P("expert", "tensor"),
        P("expert"),
        P(),
        P(),
        P("expert", "tensor", None),
        P("expert", "tensor", None),
        P("expert", "tensor", None),
    )
    out_specs = (P("tensor", "expert"), P("tensor", "expert"))
    fused = dict(mesh.shape) == {"expert": 16, "tensor": 2}
    return jax.shard_map(fused_body if fused else body, mesh=mesh, in_specs=in_specs, out_specs=out_specs, check_vma=False)
```

```python
import jax
import jax.numpy as jnp
from jax import lax
from jax.experimental import pallas as pl
from jax.experimental.pallas import tpu as pltpu
from jax.sharding import PartitionSpec as P

floor_value = -1e30
epsilon = 1e-06


def softmax_parts(queries, key_block, value_block, usable, score_scale):
    scores = (
        jnp.einsum("rkgd,rpkd->rkgp", queries, key_block, preferred_element_type=jnp.float32)
        * score_scale
    )
    usable_mask = usable[:, None, None, :]
    peak = jnp.max(jnp.where(usable_mask, scores, floor_value), axis=-1)
    raw_weights = jnp.where(usable_mask, jnp.exp(scores - peak[..., None]), 0.0)
    weight_sum = jnp.sum(raw_weights, axis=-1)
    weighted = jnp.einsum("rkgp,rpkd->rkgd", raw_weights, value_block.astype(jnp.float32))
    return (weight_sum, weighted)


def body(
    query,
    cache_keys,
    cache_values,
    lengths,
    residual,
    out_proj,
    norm_gain,
    expert_ids,
    gate_scores,
    w_gate,
    w_up,
    w_down,
):
    row_count, full_heads_width = query.shape
    cache_len = cache_keys.shape[1]
    kv_count = cache_keys.shape[2]
    head_size = cache_keys.shape[3]
    head_count = full_heads_width // head_size
    group_size = head_count // kv_count
    score_scale = head_size ** (-0.5)
    usable = jnp.arange(cache_len, dtype=jnp.int32)[None, :] < lengths[:, None]
    grouped = query.reshape(row_count, kv_count, group_size, head_size)
    weight_sum, weighted = softmax_parts(grouped, cache_keys, cache_values, usable, score_scale)
    context_rows_own = (
        (weighted / weight_sum[..., None]).astype(jnp.bfloat16).reshape(row_count, full_heads_width)
    )
    context = lax.all_to_all(context_rows_own, "tensor", split_axis=1, concat_axis=0, tiled=True)
    attn_part = jnp.dot(
        lax.all_gather(context, "expert", axis=0, tiled=True),
        out_proj.T,
        preferred_element_type=jnp.float32,
    )
    attn_share = lax.psum_scatter(attn_part, "tensor", scatter_dimension=0, tiled=True)
    hidden_state = residual.astype(jnp.float32) + attn_share
    squares = lax.psum(jnp.sum(hidden_state * hidden_state, axis=1), "expert")
    full_width = hidden_state.shape[1] * lax.axis_size("expert")
    scaled_share = (hidden_state * norm_gain.astype(jnp.float32)[None, :]).astype(jnp.bfloat16)
    scaled = lax.all_gather(
        lax.all_gather(scaled_share, "tensor", axis=0, tiled=True), "expert", axis=1, tiled=True
    )
    mean_all = lax.all_gather(squares / full_width, "tensor", axis=0, tiled=True)
    row_scale = lax.rsqrt(mean_all + epsilon)[:, None]
    experts_local = w_gate.shape[0]
    gate_weight = gate_scores.astype(jnp.float32)
    gate_weight = gate_weight / jnp.sum(gate_weight, axis=1, keepdims=True)
    mixed = None
    for local in range(experts_local):
        expert = lax.axis_index("expert") * experts_local + local
        weight = jnp.sum(jnp.where(expert_ids == expert, gate_weight, 0.0), axis=1, keepdims=True)
        gate_proj = row_scale * lax.dot_general(
            scaled, w_gate[local], (((1,), (1,)), ((), ())), preferred_element_type=jnp.float32
        )
        up_proj = row_scale * lax.dot_general(
            scaled, w_up[local], (((1,), (1,)), ((), ())), preferred_element_type=jnp.float32
        )
        activation = (jax.nn.silu(gate_proj) * up_proj).astype(jnp.bfloat16)
        part = weight * jnp.dot(activation, w_down[local], preferred_element_type=jnp.float32)
        mixed = part if mixed is None else mixed + part
    mixed = lax.psum_scatter(
        mixed.astype(jnp.bfloat16), "tensor", scatter_dimension=0, tiled=True
    )
    mixed_share = lax.psum_scatter(mixed, "expert", scatter_dimension=1, tiled=True)
    return (hidden_state.astype(jnp.bfloat16), mixed_share)


MESH = pl.DeviceIdType.MESH
NZ = 4
ACROSS, CORE = 4, 8


def remote(src, dst, send, recv, device):
    return pltpu.make_async_remote_copy(
        src_ref=src, dst_ref=dst, send_sem=send, recv_sem=recv, device_id=device, device_id_type=MESH
    )


class Net:
    def __init__(self, buf, sends, recvs, place, order):
        self.buf, self.sends, self.recvs = buf, sends, recvs
        self.z, self.x, self.c, self.y = place
        self.order = order
        self.started = []

    def slot(self, zz, xx, cc):
        return zz * 4 + xx * 2 + cc

    def copy(self, slot, half, send, recv, device):
        ref = self.buf.at[slot] if half is None else self.buf.at[slot, half]
        return remote(ref, ref, self.sends.at[send], self.recvs.at[recv], device)

    def go(self, slot, half, send, recv, device):
        copy = self.copy(slot, half, send, recv, device)
        copy.start()
        self.started.append(copy)

    def landed(self, slot, half, recv):
        e = self.slot(self.z, self.x, self.c)
        self.copy(slot, half, 0, recv, (e, 1 - self.y)).wait_recv()

    def along_z(self, half, base):
        z, x, c = self.z, self.x, self.c
        for i in range(NZ - 2, -1, -1):
            zz = self.order[i]
            self.go(self.slot(z, x, c), half, base + zz, base + z, (self.slot(zz, x, c), self.y))

    def z_landed(self, zz, half, base):
        self.landed(self.slot(zz, self.x, self.c), half, base + zz)

    def to_core(self, zz, xx, half, base):
        sem = base + xx * NZ + zz
        other = (self.slot(self.z, self.x, 1 - self.c), self.y)
        self.go(self.slot(zz, xx, self.c), half, sem, sem, other)

    def core_landed(self, zz, xx, half, base):
        self.landed(self.slot(zz, xx, 1 - self.c), half, base + xx * NZ + zz)

    def wait_sends(self):
        for copy in self.started:
            copy.wait_send()


class PlaneGather(Net):
    def onward(self, zz, k):
        half, sem = self.halves[k], 8 + k * NZ + zz
        z, x, c = self.z, self.x, self.c
        self.go(self.slot(zz, x, c), half, sem, sem, (self.slot(z, 1 - x, c), self.y))
        self.to_core(zz, x, half, 16 + 8 * k)

    def take_z(self, i, k):
        zz = self.order[NZ - 1 - i]
        self.z_landed(zz, self.halves[k], k * NZ)
        self.onward(zz, k)

    def take_x(self, i, k):
        zz = self.order[NZ - 1 - i]
        self.landed(self.slot(zz, 1 - self.x, self.c), self.halves[k], 8 + k * NZ + zz)
        self.to_core(zz, 1 - self.x, self.halves[k], 16 + 8 * k)

    def begin(self):
        self.halves = (self.y, 1 - self.y)
        self.along_z(self.halves[0], 0)
        self.onward(self.z, 0)

    def middle(self, swap):
        swap.wait_recv()
        self.along_z(self.halves[1], NZ)
        self.onward(self.z, 1)
        for i in range(1, NZ):
            self.take_z(i, 0)
        self.take_x(0, 0)
        for i in range(1, NZ):
            self.take_z(i, 1)
            self.take_x(i, 0)

    def wait_core(self, k):
        for zz in range(NZ):
            for xx in range(2):
                self.core_landed(zz, xx, self.halves[k], 16 + 8 * k)


class QuadGather(Net):
    def onward(self, zz):
        z, x, c, y = self.z, self.x, self.c, self.y
        own, across = self.slot(z, x, c), self.slot(z, 1 - x, c)
        src = self.slot(zz, x, c)
        self.go(src, 1 - y, 4 + zz, 4 + zz, (across, 1 - y))
        self.go(src, 1 - y, 8 + zz, 8 + zz, (across, y))
        self.go(src, 1 - y, 12 + zz, 12 + zz, (own, 1 - y))

    def begin(self):
        self.along_z(1 - self.y, 0)
        self.onward(self.z)

    def take_z(self, i):
        zz = self.order[NZ - 1 - i]
        self.z_landed(zz, 1 - self.y, 0)
        self.onward(zz)

    def take_level(self, i):
        zz = self.order[NZ - 1 - i]
        near, far = self.slot(zz, self.x, self.c), self.slot(zz, 1 - self.x, self.c)
        self.landed(near, self.y, 12 + zz)
        self.to_core(zz, self.x, None, 16)
        self.landed(far, 1 - self.y, 8 + zz)
        self.landed(far, self.y, 4 + zz)
        self.to_core(zz, 1 - self.x, None, 16)
        return [near, far]

    def take_core(self, i):
        zz = self.order[NZ - 1 - i]
        for xx in (self.x, 1 - self.x):
            self.core_landed(zz, xx, None, 16)
        return [self.slot(zz, self.x, 1 - self.c), self.slot(zz, 1 - self.x, 1 - self.c)]


def nt_dot(a, b):
    return lax.dot_general(a, b, (((1,), (1,)), ((), ())), preferred_element_type=jnp.float32)


def low_rows(rows):
    return (lax.broadcasted_iota(jnp.int32, (rows, 256), 0) % 8) < 4


def up4(a):
    return pltpu.roll(a, a.shape[0] - 4, 0)


def down4(a):
    return pltpu.roll(a, 4, 0)


def interleave(a, b):
    rows, low = a.shape[0], low_rows(a.shape[0])
    even = jnp.where(low, a, down4(b)).reshape(rows // 8, 1, 8, 256)
    odd = jnp.where(low, up4(a), b).reshape(rows // 8, 1, 8, 256)
    return jnp.concatenate([even, odd], axis=1).reshape(2 * rows, 256)


def layer_kernel(
    q_hbm, k_hbm, v_hbm, len_ref, res_hbm, wo_hbm, gain_hbm, ids_hbm, gates_hbm,
    wg_hbm, wu_hbm, wd_hbm,
    out_ref,
    q_ref, res_ref, gain_ref, ids_ref, gates_ref,
    k_v, v_v, wo_v, wg_v, wu_v, wd_v, local_sems,
    lay, qlay, sblk, ctx, part_out, part_in, res_part, res_all, hid_own, hid_rows, hid_all, sq_own, sq_level, sq_total, sq_in, sq_z,
    gate_acc, up_acc, act, mine, core_out, core_in, x_out, x_in, y_out, y_in, d_out, d_in, z_out, z_in,
    c_send, c_recv, h_send, h_recv, p_send, p_recv, q_send, q_recv, r_send, r_recv,
):
    f32, bf16 = jnp.float32, jnp.bfloat16
    e = lax.axis_index("expert")
    y = lax.axis_index("tensor")
    z, x, c = e // 4, (e // 2) % 2, e % 2
    ex, ec = e + 2 * (1 - 2 * x), e + 1 - 2 * c
    mirror = z // 2
    near_z = z + mirror * (3 - 2 * z)
    order = [o + mirror * (3 - 2 * o) for o in (3, 2, 1 - near_z, near_z)]
    barrier = pltpu.get_barrier_semaphore()
    pairs = [(k_hbm, k_v), (v_hbm, v_v), (wo_hbm, wo_v), (wg_hbm, wg_v), (wu_hbm, wu_v), (wd_hbm, wd_v)]
    pairs += [(q_hbm, q_ref), (res_hbm, res_ref), (gain_hbm, gain_ref), (ids_hbm, ids_ref), (gates_hbm, gates_ref)]
    loads = [pltpu.make_async_copy(s, d, local_sems.at[i]) for i, (s, d) in enumerate(pairs)]
    first = [loads[6], loads[0], loads[1]] + loads[7:]
    for d in first:
        d.start()
    peers = [(ec, y), (ex, y), (e, 1 - y), (ex, 1 - y)]
    peers += [(order[i] * 4 + x * 2 + c, y) for i in range(NZ - 1)]
    for dev in peers:
        pl.semaphore_signal(barrier, inc=1, device_id=dev, device_id_type=MESH)

    rows = q_ref.shape[0]
    col = lax.broadcasted_iota(jnp.int32, (64, 512), 1)
    head = lax.broadcasted_iota(jnp.int32, (64, 512), 0)
    same = (col % 4) == (head // 16)
    loads[6].wait()
    for h in range(64):
        qlay[h * 8 : h * 8 + rows, :] = q_ref[:, h * 128 : (h + 1) * 128].astype(f32)
    loads[0].wait()
    loads[1].wait()
    for d in loads[2:6]:
        d.start()
    scores, weights, totals = [], [], []
    for r in range(rows):
        q = qlay[pl.ds(r, 64, stride=8), :].astype(bf16)
        s = nt_dot(q, k_v[r]) * (128 ** -0.5)
        scores.append(jnp.where(same & ((col // 4) < len_ref[r]), s, -1e30))
    for s in scores:
        w = jnp.exp(s - jnp.max(s, axis=1, keepdims=True))
        totals.append(jnp.sum(w, axis=1, keepdims=True))
        weights.append(w.astype(bf16))
    for r in range(rows):
        o = jnp.dot(weights[r], v_v[r], preferred_element_type=f32) / totals[r]
        for half in range(2):
            for j in range(4):
                h0 = half * 32 + j * 8
                lay[pl.ds(half * 128 + 4 * j + r, 8, stride=16), :] = o[h0 : h0 + 8]
    for half in range(2):
        for hh in range(8):
            t = (half * 8 + hh) * 16
            sblk[half, :, hh * 128 : (hh + 1) * 128] = lay[t : t + 16, :].astype(bf16)
    ctx[e, y] = sblk[y]
    pl.semaphore_wait(barrier, 7)

    swap = remote(sblk.at[1 - y], ctx.at[e, y], p_send.at[0], p_recv.at[0], (e, 1 - y))
    swap.start()
    g1 = PlaneGather(ctx, c_send, c_recv, (z, x, c, y), order)
    g1.begin()
    for d in loads[7:]:
        d.wait()
    tiles = res_ref[...].astype(f32).reshape(4, 2, 8, 256)
    even, odd = tiles[:, 0].reshape(32, 256), tiles[:, 1].reshape(32, 256)
    res_part[0] = jnp.where(low_rows(32), even, down4(odd)).astype(bf16)
    res_part[1] = jnp.where(low_rows(32), up4(even), odd).astype(bf16)
    res_all[y] = res_part[1 - y]
    rsend = remote(res_part.at[y], res_all.at[y], p_send.at[2], p_recv.at[2], (e, 1 - y))
    rsend.start()
    g1.middle(swap)
    loads[2].wait()
    quarter = (lax.broadcasted_iota(jnp.int32, (256, 256), 0) % 16) // 4
    low = (lax.broadcasted_iota(jnp.int32, (128, 256), 0) % 8) < 4
    low3 = lax.broadcasted_iota(jnp.int32, (8, 8, 256), 1) < 4

    def attn_half(h):
        lhs = ctx[:, h].reshape(256, 1024)
        acc = jnp.zeros((256, 256), f32)
        for j in range(4):
            pj = nt_dot(lhs, wo_v[:, j * 1024 : (j + 1) * 1024])
            acc = jnp.where(quarter == j, pj, acc)
        folded = acc.reshape(16, 2, 8, 256)
        folded = (folded[:, 0] + folded[:, 1]).reshape(128, 256)
        folded = folded + jnp.where(low, pltpu.roll(folded, 124, 0), pltpu.roll(folded, 4, 0))
        folded = folded.reshape(8, 2, 8, 256)
        return jnp.where(low3, folded[:, 0], folded[:, 1]).reshape(64, 256)

    g1.wait_core(0)
    part_out[...] = attn_half(y).astype(bf16)
    psend = remote(part_out, part_in, p_send.at[1], p_recv.at[1], (e, 1 - y))
    psend.start()
    g1.take_x(0, 1)
    g1.take_x(1, 1)
    g1.take_x(2, 1)
    g1.take_x(3, 1)
    g1.wait_core(1)
    mine_part = attn_half(1 - y)
    rsend.wait_recv()
    psend.wait_recv()
    hidden = res_all[...].reshape(64, 256).astype(f32) + (mine_part + part_in[...].astype(f32))
    hid_all[e, 1 - y] = (hidden * gain_ref[...].astype(f32).reshape(1, 256)).astype(bf16)
    g2 = QuadGather(hid_all, h_send, h_recv, (z, x, c, y), order)
    g2.begin()
    ss = jnp.sum(hidden * hidden, axis=1, keepdims=True)
    spot = lax.broadcasted_iota(jnp.int32, (64, 128), 0) + 64 * (1 - y)
    lane = lax.broadcasted_iota(jnp.int32, (64, 128), 1)
    sq = jnp.sum(jnp.where(spot == lane, ss, 0.0), axis=0, keepdims=True)
    sq_own[...] = jnp.broadcast_to(sq, (8, 128))
    sq_core = remote(sq_own, sq_in.at[0], q_send.at[0], q_recv.at[0], (ec, y))
    sq_core.start()
    sq_core.wait_recv()
    sq_level[...] = sq_own[...] + sq_in[0]
    sq_quad = [
        remote(sq_level, sq_in.at[k], q_send.at[k], q_recv.at[k], dev)
        for k, dev in ((1, (ex, y)), (2, (e, 1 - y)), (3, (ex, 1 - y)))
    ]
    for copy in sq_quad:
        copy.start()
    swap.wait_send()
    psend.wait_send()
    g1.wait_sends()
    hid_own[...] = hidden.astype(bf16).reshape(2, 32, 256)
    hid_rows[1 - y] = hid_own[y]
    osend = remote(hid_own.at[1 - y], hid_rows.at[1 - y], p_send.at[3], p_recv.at[3], (e, 1 - y))
    osend.start()
    eye = lax.broadcasted_iota(jnp.int32, (128, 128), 0) == lax.broadcasted_iota(jnp.int32, (128, 128), 1)
    gw = gates_ref[...].astype(f32)
    gw = gw / jnp.sum(gw, axis=0, keepdims=True)
    weight_row = jnp.sum(jnp.where(ids_ref[...] == e, gw, 0.0), axis=0, keepdims=True)
    spot = lax.broadcasted_iota(jnp.int32, (128, 128), 0)
    row = (spot % 64) // 4 * 8 + spot // 64 * 4 + spot % 4
    named = row == lax.broadcasted_iota(jnp.int32, (128, 128), 1)
    weight = jnp.sum(jnp.where(named, weight_row, 0.0), axis=1, keepdims=True)

    def products(slots, first=False):
        for n in range(3):
            for wref, aref in ((wg_v, gate_acc), (wu_v, up_acc)):
                a = None if first else aref[n]
                for src in slots:
                    cols = pl.ds(pl.multiple_of(src * 256, 256), 256)
                    t = nt_dot(hid_all[src].reshape(128, 256), wref[n * 256 : (n + 1) * 256, cols])
                    a = t if a is None else a + t
                aref[n] = a

    for i in range(1, NZ):
        g2.take_z(i)
    loads[3].wait()
    loads[4].wait()
    slots = g2.take_level(0)
    for copy in sq_quad:
        copy.wait_recv()
    sq_total[...] = (sq_level[...] + sq_in[1]) + (sq_in[2] + sq_in[3])

    def sq_z_copy(zz):
        return remote(
            sq_total, sq_z.at[z], q_send.at[4 + zz], q_recv.at[4 + z], (zz * 4 + x * 2 + c, y)
        )

    def sq_z_landing(zz):
        return remote(
            sq_total, sq_z.at[zz], q_send.at[4 + z], q_recv.at[4 + zz], (zz * 4 + x * 2 + c, y)
        )

    for i in range(NZ - 1):
        sq_z_copy(order[i]).start()
    products(slots, True)
    for i in range(1, NZ):
        products(g2.take_level(i) + g2.take_core(i - 1))
    products(g2.take_core(NZ - 1))

    total = sq_total[...]
    for i in range(NZ - 1):
        sq_z_landing(order[i]).wait_recv()
        total = total + sq_z[order[i]]
    scale_row = lax.rsqrt(total[0:1] / 4096.0 + epsilon)
    scale = jnp.sum(jnp.where(eye, scale_row, 0.0), axis=1, keepdims=True)
    for n in range(3):
        g = gate_acc[n] * scale
        u = up_acc[n] * scale
        a = g / (1.0 + jnp.exp(-g)) * u * weight
        a = interleave(a[0:64], a[64:128]).astype(bf16)
        for half in range(2):
            to = pl.ds(pl.multiple_of(((half + y) % 2) * 64, 64), 64)
            act[to, n * 256 : (n + 1) * 256] = a[half * 64 : (half + 1) * 64]
    loads[5].wait()

    def block(zz, xx, cc):
        cols = pl.ds(pl.multiple_of((zz * 4 + xx * 2 + cc) * 256, 256), 256)
        return jnp.dot(act[...], wd_v[:, cols], preferred_element_type=f32)

    def core_copy(zz, k):
        b = k * NZ + zz
        return remote(core_out.at[b], core_in.at[b], r_send.at[b], r_recv.at[b], (ec, y))

    def x_copy(zz):
        return remote(x_out.at[zz], x_in.at[zz], r_send.at[8 + zz], r_recv.at[8 + zz], (ex, y))

    def y_copy(zz):
        return remote(y_out.at[zz], y_in.at[zz], r_send.at[12 + zz], r_recv.at[12 + zz], (e, 1 - y))

    def d_copy(zz):
        return remote(d_out.at[zz], d_in.at[zz], r_send.at[16 + zz], r_recv.at[16 + zz], (ex, 1 - y))

    def z_copy(zz):
        return remote(
            z_out.at[zz], z_in.at[z], r_send.at[20 + zz], r_recv.at[20 + z], (zz * 4 + x * 2 + c, y)
        )

    def z_landing(zz):
        return remote(
            z_out.at[zz], z_in.at[zz], r_send.at[20 + z], r_recv.at[20 + zz], (zz * 4 + x * 2 + c, y)
        )

    def to_core(zz):
        blocks = [block(zz, xx, 1 - c).astype(bf16) for xx in (1 - x, x)]
        for k in range(2):
            core_out[k * NZ + zz] = blocks[k]
            core_copy(zz, k).start()

    def to_plane(zz):
        far = block(zz, 1 - x, c)
        core_copy(zz, 0).wait_recv()
        far = far + core_in[zz].astype(f32)
        d_out[zz] = far[64:128].astype(bf16)
        d_copy(zz).start()
        x_out[zz] = far[0:64].astype(bf16)
        x_copy(zz).start()
        near = block(zz, x, c)
        core_copy(zz, 1).wait_recv()
        near = near + core_in[NZ + zz].astype(f32)
        y_out[zz] = near[64:128].astype(bf16)
        y_copy(zz).start()
        mine[zz] = near[0:64]

    def plane_sum(zz):
        x_copy(zz).wait_recv()
        y_copy(zz).wait_recv()
        d_copy(zz).wait_recv()
        return mine[zz] + x_in[zz].astype(f32) + (y_in[zz].astype(f32) + d_in[zz].astype(f32))

    to_core(order[0])
    for i in range(NZ):
        if i < NZ - 1:
            to_core(order[i + 1])
        if i == NZ - 1:
            g2.wait_sends()
            rsend.wait_send()
            osend.wait_send()
            osend.wait_recv()
            out_ref[0] = interleave(hid_rows[0].astype(f32), hid_rows[1].astype(f32)).astype(bf16)
            for copy in [sq_core] + sq_quad + [sq_z_copy(order[i]) for i in range(NZ - 1)]:
                copy.wait_send()
        to_plane(order[i])
    for i in range(NZ - 1):
        zz = order[i]
        z_out[zz] = plane_sum(zz).astype(bf16)
        z_copy(zz).start()
        for copy in (core_copy(zz, 0), core_copy(zz, 1), x_copy(zz), y_copy(zz), d_copy(zz)):
            copy.wait_send()
    fin = plane_sum(z)
    for copy in (core_copy(z, 0), core_copy(z, 1), x_copy(z), y_copy(z), d_copy(z)):
        copy.wait_send()
    for i in range(NZ - 1):
        z_copy(order[i]).wait_send()
    for i in range(NZ - 2, -1, -1):
        zz = order[i]
        z_landing(zz).wait_recv()
        fin = fin + z_in[zz].astype(f32)
    out_ref[1] = fin.astype(bf16)


def fused_body(
    query, cache_keys, cache_values, lengths, residual, out_proj, norm_gain, expert_ids, gate_scores,
    w_gate, w_up, w_down,
):
    f32, bf16 = jnp.float32, jnp.bfloat16
    rows = query.shape[0]
    keys = cache_keys.reshape(rows, 512, 128)
    values = cache_values.reshape(rows, 512, 128)
    vm = pl.BlockSpec(memory_space=pltpu.VMEM)
    hb = pl.BlockSpec(memory_space=pl.ANY)
    sm = pl.BlockSpec(memory_space=pltpu.SMEM)
    V, S = pltpu.VMEM, pltpu.SemaphoreType.DMA
    out = pl.pallas_call(
        layer_kernel,
        name="layer",
        out_shape=pltpu.VMEM((2, 64, 256), bf16),
        in_specs=[hb, hb, hb, sm, hb, hb, hb, hb, hb, hb, hb, hb],
        out_specs=vm,
        scratch_shapes=[
            V((rows, 8192), bf16), V((64, 256), bf16), V((256,), bf16), V((8, 128), jnp.int32), V((8, 128), bf16),
            V((rows, 512, 128), bf16), V((rows, 512, 128), bf16), V((256, 4096), bf16),
            V((768, 4096), bf16), V((768, 4096), bf16), V((768, 4096), bf16), S((11,)),
            V((256, 128), f32), V((512, 128), f32), V((2, 16, 1024), bf16), V((16, 2, 16, 1024), bf16),
            V((64, 256), bf16), V((64, 256), bf16),
            V((2, 32, 256), bf16), V((2, 32, 256), bf16), V((2, 32, 256), bf16), V((2, 32, 256), bf16),
            V((16, 2, 64, 256), bf16),
            V((8, 128), f32), V((8, 128), f32), V((8, 128), f32), V((4, 8, 128), f32), V((4, 8, 128), f32),
            V((3, 128, 256), f32), V((3, 128, 256), f32), V((128, 768), bf16),
            V((4, 64, 256), f32), V((8, 128, 256), bf16), V((8, 128, 256), bf16),
            V((4, 64, 256), bf16), V((4, 64, 256), bf16), V((4, 64, 256), bf16), V((4, 64, 256), bf16),
            V((4, 64, 256), bf16), V((4, 64, 256), bf16), V((4, 64, 256), bf16), V((4, 64, 256), bf16),
            S((32,)), S((32,)), S((24,)), S((24,)), S((4,)), S((4,)), S((8,)), S((8,)), S((24,)), S((24,)),
        ],
        compiler_params=pltpu.CompilerParams(
            collective_id=0, has_side_effects=True, vmem_limit_bytes=62 * 1024 * 1024
        ),
    )(
        query, keys, values, lengths, residual, out_proj, norm_gain, expert_ids.T,
        gate_scores.T, w_gate[0], w_up[0], w_down[0],
    )
    return (out[0], out[1])


def solution(mesh):
    in_specs = (
        P(("expert", "tensor"), None),
        P(("expert", "tensor"), None, None, None),
        P(("expert", "tensor"), None, None, None),
        P(("expert", "tensor")),
        P("tensor", "expert"),
        P("expert", "tensor"),
        P("expert"),
        P(),
        P(),
        P("expert", "tensor", None),
        P("expert", "tensor", None),
        P("expert", "tensor", None),
    )
    out_specs = (P("tensor", "expert"), P("tensor", "expert"))
    fused = dict(mesh.shape) == {"expert": 16, "tensor": 2}
    return jax.shard_map(fused_body if fused else body, mesh=mesh, in_specs=in_specs, out_specs=out_specs, check_vma=False)
```

```python
import jax
import jax.numpy as jnp
from jax import lax
from jax.experimental import pallas as pl
from jax.experimental.pallas import tpu as pltpu
from jax.sharding import PartitionSpec as P

floor_value = -1e30
epsilon = 1e-06


def softmax_parts(queries, key_block, value_block, usable, score_scale):
    scores = (
        jnp.einsum("rkgd,rpkd->rkgp", queries, key_block, preferred_element_type=jnp.float32)
        * score_scale
    )
    usable_mask = usable[:, None, None, :]
    peak = jnp.max(jnp.where(usable_mask, scores, floor_value), axis=-1)
    raw_weights = jnp.where(usable_mask, jnp.exp(scores - peak[..., None]), 0.0)
    weight_sum = jnp.sum(raw_weights, axis=-1)
    weighted = jnp.einsum("rkgp,rpkd->rkgd", raw_weights, value_block.astype(jnp.float32))
    return (weight_sum, weighted)


def body(
    query,
    cache_keys,
    cache_values,
    lengths,
    residual,
    out_proj,
    norm_gain,
    expert_ids,
    gate_scores,
    w_gate,
    w_up,
    w_down,
):
    row_count, full_heads_width = query.shape
    cache_len = cache_keys.shape[1]
    kv_count = cache_keys.shape[2]
    head_size = cache_keys.shape[3]
    head_count = full_heads_width // head_size
    group_size = head_count // kv_count
    score_scale = head_size ** (-0.5)
    usable = jnp.arange(cache_len, dtype=jnp.int32)[None, :] < lengths[:, None]
    grouped = query.reshape(row_count, kv_count, group_size, head_size)
    weight_sum, weighted = softmax_parts(grouped, cache_keys, cache_values, usable, score_scale)
    context_rows_own = (
        (weighted / weight_sum[..., None]).astype(jnp.bfloat16).reshape(row_count, full_heads_width)
    )
    context = lax.all_to_all(context_rows_own, "tensor", split_axis=1, concat_axis=0, tiled=True)
    attn_part = jnp.dot(
        lax.all_gather(context, "expert", axis=0, tiled=True),
        out_proj.T,
        preferred_element_type=jnp.float32,
    )
    attn_share = lax.psum_scatter(attn_part, "tensor", scatter_dimension=0, tiled=True)
    hidden_state = residual.astype(jnp.float32) + attn_share
    squares = lax.psum(jnp.sum(hidden_state * hidden_state, axis=1), "expert")
    full_width = hidden_state.shape[1] * lax.axis_size("expert")
    scaled_share = (hidden_state * norm_gain.astype(jnp.float32)[None, :]).astype(jnp.bfloat16)
    scaled = lax.all_gather(
        lax.all_gather(scaled_share, "tensor", axis=0, tiled=True), "expert", axis=1, tiled=True
    )
    mean_all = lax.all_gather(squares / full_width, "tensor", axis=0, tiled=True)
    row_scale = lax.rsqrt(mean_all + epsilon)[:, None]
    experts_local = w_gate.shape[0]
    gate_weight = gate_scores.astype(jnp.float32)
    gate_weight = gate_weight / jnp.sum(gate_weight, axis=1, keepdims=True)
    mixed = None
    for local in range(experts_local):
        expert = lax.axis_index("expert") * experts_local + local
        weight = jnp.sum(jnp.where(expert_ids == expert, gate_weight, 0.0), axis=1, keepdims=True)
        gate_proj = row_scale * lax.dot_general(
            scaled, w_gate[local], (((1,), (1,)), ((), ())), preferred_element_type=jnp.float32
        )
        up_proj = row_scale * lax.dot_general(
            scaled, w_up[local], (((1,), (1,)), ((), ())), preferred_element_type=jnp.float32
        )
        activation = (jax.nn.silu(gate_proj) * up_proj).astype(jnp.bfloat16)
        part = weight * jnp.dot(activation, w_down[local], preferred_element_type=jnp.float32)
        mixed = part if mixed is None else mixed + part
    mixed = lax.psum_scatter(
        mixed.astype(jnp.bfloat16), "tensor", scatter_dimension=0, tiled=True
    )
    mixed_share = lax.psum_scatter(mixed, "expert", scatter_dimension=1, tiled=True)
    return (hidden_state.astype(jnp.bfloat16), mixed_share)


MESH = pl.DeviceIdType.MESH
NZ = 4
ACROSS, CORE = 4, 8


def remote(src, dst, send, recv, device):
    return pltpu.make_async_remote_copy(
        src_ref=src, dst_ref=dst, send_sem=send, recv_sem=recv, device_id=device, device_id_type=MESH
    )


class Net:
    def __init__(self, buf, sends, recvs, place, order):
        self.buf, self.sends, self.recvs = buf, sends, recvs
        self.z, self.x, self.c, self.y = place
        self.order = order
        self.started = []

    def slot(self, zz, xx, cc):
        return zz * 4 + xx * 2 + cc

    def copy(self, slot, half, send, recv, device):
        ref = self.buf.at[slot] if half is None else self.buf.at[slot, half]
        return remote(ref, ref, self.sends.at[send], self.recvs.at[recv], device)

    def go(self, slot, half, send, recv, device):
        copy = self.copy(slot, half, send, recv, device)
        copy.start()
        self.started.append(copy)

    def landed(self, slot, half, recv):
        e = self.slot(self.z, self.x, self.c)
        self.copy(slot, half, 0, recv, (e, 1 - self.y)).wait_recv()

    def along_z(self, half, base):
        z, x, c = self.z, self.x, self.c
        for i in range(NZ - 2, -1, -1):
            zz = self.order[i]
            self.go(self.slot(z, x, c), half, base + zz, base + z, (self.slot(zz, x, c), self.y))

    def z_landed(self, zz, half, base):
        self.landed(self.slot(zz, self.x, self.c), half, base + zz)

    def to_core(self, zz, xx, half, base):
        sem = base + xx * NZ + zz
        other = (self.slot(self.z, self.x, 1 - self.c), self.y)
        self.go(self.slot(zz, xx, self.c), half, sem, sem, other)

    def core_landed(self, zz, xx, half, base):
        self.landed(self.slot(zz, xx, 1 - self.c), half, base + xx * NZ + zz)

    def wait_sends(self):
        for copy in self.started:
            copy.wait_send()


class PlaneGather(Net):
    def onward(self, zz, k):
        half, sem = self.halves[k], 8 + k * NZ + zz
        z, x, c = self.z, self.x, self.c
        self.go(self.slot(zz, x, c), half, sem, sem, (self.slot(z, 1 - x, c), self.y))
        self.to_core(zz, x, half, 16 + 8 * k)

    def take_z(self, i, k):
        zz = self.order[NZ - 1 - i]
        self.z_landed(zz, self.halves[k], k * NZ)
        self.onward(zz, k)

    def take_x(self, i, k):
        zz = self.order[NZ - 1 - i]
        self.landed(self.slot(zz, 1 - self.x, self.c), self.halves[k], 8 + k * NZ + zz)
        self.to_core(zz, 1 - self.x, self.halves[k], 16 + 8 * k)

    def begin(self):
        self.halves = (self.y, 1 - self.y)
        self.along_z(self.halves[0], 0)
        self.onward(self.z, 0)

    def middle(self, swap):
        swap.wait_recv()
        self.along_z(self.halves[1], NZ)
        self.onward(self.z, 1)
        for i in range(1, NZ):
            self.take_z(i, 0)
        self.take_x(0, 0)
        for i in range(1, NZ):
            self.take_z(i, 1)
            self.take_x(i, 0)

    def wait_core(self, k):
        for zz in range(NZ):
            for xx in range(2):
                self.core_landed(zz, xx, self.halves[k], 16 + 8 * k)


class QuadGather(Net):
    def onward(self, zz):
        z, x, c, y = self.z, self.x, self.c, self.y
        own, across = self.slot(z, x, c), self.slot(z, 1 - x, c)
        src = self.slot(zz, x, c)
        self.go(src, 1 - y, 4 + zz, 4 + zz, (across, 1 - y))
        self.go(src, 1 - y, 8 + zz, 8 + zz, (across, y))
        self.go(src, 1 - y, 12 + zz, 12 + zz, (own, 1 - y))

    def begin(self):
        self.along_z(1 - self.y, 0)
        self.onward(self.z)

    def take_z(self, i):
        zz = self.order[NZ - 1 - i]
        self.z_landed(zz, 1 - self.y, 0)
        self.onward(zz)

    def take_level(self, i):
        zz = self.order[NZ - 1 - i]
        near, far = self.slot(zz, self.x, self.c), self.slot(zz, 1 - self.x, self.c)
        self.landed(near, self.y, 12 + zz)
        self.to_core(zz, self.x, None, 16)
        self.landed(far, 1 - self.y, 8 + zz)
        self.landed(far, self.y, 4 + zz)
        self.to_core(zz, 1 - self.x, None, 16)
        return [near, far]

    def take_core(self, i):
        zz = self.order[NZ - 1 - i]
        for xx in (self.x, 1 - self.x):
            self.core_landed(zz, xx, None, 16)
        return [self.slot(zz, self.x, 1 - self.c), self.slot(zz, 1 - self.x, 1 - self.c)]


def nt_dot(a, b):
    return lax.dot_general(a, b, (((1,), (1,)), ((), ())), preferred_element_type=jnp.float32)


def low_rows(rows):
    return (lax.broadcasted_iota(jnp.int32, (rows, 256), 0) % 8) < 4


def up4(a):
    return pltpu.roll(a, a.shape[0] - 4, 0)


def down4(a):
    return pltpu.roll(a, 4, 0)


def interleave(a, b):
    rows, low = a.shape[0], low_rows(a.shape[0])
    even = jnp.where(low, a, down4(b)).reshape(rows // 8, 1, 8, 256)
    odd = jnp.where(low, up4(a), b).reshape(rows // 8, 1, 8, 256)
    return jnp.concatenate([even, odd], axis=1).reshape(2 * rows, 256)


def layer_kernel(
    q_hbm, k_hbm, v_hbm, len_ref, res_hbm, wo_hbm, gain_hbm, ids_hbm, gates_hbm,
    wg_hbm, wu_hbm, wd_hbm,
    out_ref,
    q_ref, res_ref, gain_ref, ids_ref, gates_ref,
    k_v, v_v, wo_v, wg_v, wu_v, wd_v, local_sems,
    lay, qlay, sblk, ctx, part_out, part_in, res_part, res_all, hid_own, hid_rows, hid_all, sq_own, sq_level, sq_total, sq_in, sq_z,
    gate_acc, up_acc, act, mine, core_out, core_in, x_out, x_in, y_out, y_in, d_out, d_in, z_out, z_in,
    c_send, c_recv, h_send, h_recv, p_send, p_recv, q_send, q_recv, r_send, r_recv,
):
    f32, bf16 = jnp.float32, jnp.bfloat16
    e = lax.axis_index("expert")
    y = lax.axis_index("tensor")
    z, x, c = e // 4, (e // 2) % 2, e % 2
    ex, ec = e + 2 * (1 - 2 * x), e + 1 - 2 * c
    mirror = z // 2
    near_z = z + mirror * (3 - 2 * z)
    order = [o + mirror * (3 - 2 * o) for o in (3, 2, 1 - near_z, near_z)]
    barrier = pltpu.get_barrier_semaphore()
    pairs = [(k_hbm, k_v), (v_hbm, v_v), (wo_hbm, wo_v), (wg_hbm, wg_v), (wu_hbm, wu_v), (wd_hbm, wd_v)]
    pairs += [(q_hbm, q_ref), (res_hbm, res_ref), (gain_hbm, gain_ref), (ids_hbm, ids_ref), (gates_hbm, gates_ref)]
    loads = [pltpu.make_async_copy(s, d, local_sems.at[i]) for i, (s, d) in enumerate(pairs)]
    first = [loads[6], loads[0], loads[1]] + loads[7:]
    for d in first:
        d.start()
    peers = [(ec, y), (ex, y), (e, 1 - y), (ex, 1 - y)]
    peers += [(order[i] * 4 + x * 2 + c, y) for i in range(NZ - 1)]
    for dev in peers:
        pl.semaphore_signal(barrier, inc=1, device_id=dev, device_id_type=MESH)

    rows = q_ref.shape[0]
    col = lax.broadcasted_iota(jnp.int32, (64, 512), 1)
    head = lax.broadcasted_iota(jnp.int32, (64, 512), 0)
    same = (col % 4) == (head // 16)
    loads[6].wait()
    for h in range(64):
        qlay[h * 8 : h * 8 + rows, :] = q_ref[:, h * 128 : (h + 1) * 128].astype(f32)
    loads[0].wait()
    loads[1].wait()
    for d in loads[2:6]:
        d.start()
    scores, weights, totals = [], [], []
    for r in range(rows):
        q = qlay[pl.ds(r, 64, stride=8), :].astype(bf16)
        s = nt_dot(q, k_v[r]) * (128 ** -0.5)
        scores.append(jnp.where(same & ((col // 4) < len_ref[r]), s, -1e30))
    for s in scores:
        w = jnp.exp(s - jnp.max(s, axis=1, keepdims=True))
        totals.append(jnp.sum(w, axis=1, keepdims=True))
        weights.append(w.astype(bf16))
    for r in range(rows):
        o = jnp.dot(weights[r], v_v[r], preferred_element_type=f32) / totals[r]
        for half in range(2):
            for j in range(4):
                h0 = half * 32 + j * 8
                lay[pl.ds(half * 128 + 4 * j + r, 8, stride=16), :] = o[h0 : h0 + 8]
    for half in range(2):
        for hh in range(8):
            t = (half * 8 + hh) * 16
            sblk[half, :, hh * 128 : (hh + 1) * 128] = lay[t : t + 16, :].astype(bf16)
    ctx[e, y] = sblk[y]
    pl.semaphore_wait(barrier, 7)

    swap = remote(sblk.at[1 - y], ctx.at[e, y], p_send.at[0], p_recv.at[0], (e, 1 - y))
    swap.start()
    g1 = PlaneGather(ctx, c_send, c_recv, (z, x, c, y), order)
    g1.begin()
    for d in loads[7:]:
        d.wait()
    tiles = res_ref[...].astype(f32).reshape(4, 2, 8, 256)
    even, odd = tiles[:, 0].reshape(32, 256), tiles[:, 1].reshape(32, 256)
    res_part[0] = jnp.where(low_rows(32), even, down4(odd)).astype(bf16)
    res_part[1] = jnp.where(low_rows(32), up4(even), odd).astype(bf16)
    res_all[y] = res_part[1 - y]
    rsend = remote(res_part.at[y], res_all.at[y], p_send.at[2], p_recv.at[2], (e, 1 - y))
    rsend.start()
    g1.middle(swap)
    loads[2].wait()
    quarter = (lax.broadcasted_iota(jnp.int32, (256, 256), 0) % 16) // 4
    low = (lax.broadcasted_iota(jnp.int32, (128, 256), 0) % 8) < 4
    low3 = lax.broadcasted_iota(jnp.int32, (8, 8, 256), 1) < 4

    def attn_half(h):
        lhs = ctx[:, h].reshape(256, 1024)
        acc = jnp.zeros((256, 256), f32)
        for j in range(4):
            pj = nt_dot(lhs, wo_v[:, j * 1024 : (j + 1) * 1024])
            acc = jnp.where(quarter == j, pj, acc)
        folded = acc.reshape(16, 2, 8, 256)
        folded = (folded[:, 0] + folded[:, 1]).reshape(128, 256)
        folded = folded + jnp.where(low, pltpu.roll(folded, 124, 0), pltpu.roll(folded, 4, 0))
        folded = folded.reshape(8, 2, 8, 256)
        return jnp.where(low3, folded[:, 0], folded[:, 1]).reshape(64, 256)

    g1.wait_core(0)
    part_out[...] = attn_half(y).astype(bf16)
    psend = remote(part_out, part_in, p_send.at[1], p_recv.at[1], (e, 1 - y))
    psend.start()
    g1.take_x(0, 1)
    g1.take_x(1, 1)
    g1.take_x(2, 1)
    g1.take_x(3, 1)
    g1.wait_core(1)
    mine_part = attn_half(1 - y)
    rsend.wait_recv()
    psend.wait_recv()
    hidden = res_all[...].reshape(64, 256).astype(f32) + (mine_part + part_in[...].astype(f32))
    hid_all[e, 1 - y] = (hidden * gain_ref[...].astype(f32).reshape(1, 256)).astype(bf16)
    g2 = QuadGather(hid_all, h_send, h_recv, (z, x, c, y), order)
    g2.begin()
    ss = jnp.sum(hidden * hidden, axis=1, keepdims=True)
    spot = lax.broadcasted_iota(jnp.int32, (64, 128), 0) + 64 * (1 - y)
    lane = lax.broadcasted_iota(jnp.int32, (64, 128), 1)
    sq = jnp.sum(jnp.where(spot == lane, ss, 0.0), axis=0, keepdims=True)
    sq_own[...] = jnp.broadcast_to(sq, (8, 128))
    sq_core = remote(sq_own, sq_in.at[0], q_send.at[0], q_recv.at[0], (ec, y))
    sq_core.start()
    sq_core.wait_recv()
    sq_level[...] = sq_own[...] + sq_in[0]
    sq_quad = [
        remote(sq_level, sq_in.at[k], q_send.at[k], q_recv.at[k], dev)
        for k, dev in ((1, (ex, y)), (2, (e, 1 - y)), (3, (ex, 1 - y)))
    ]
    for copy in sq_quad:
        copy.start()
    swap.wait_send()
    psend.wait_send()
    g1.wait_sends()
    hid_own[...] = hidden.astype(bf16).reshape(2, 32, 256)
    hid_rows[1 - y] = hid_own[y]
    osend = remote(hid_own.at[1 - y], hid_rows.at[1 - y], p_send.at[3], p_recv.at[3], (e, 1 - y))
    osend.start()
    eye = lax.broadcasted_iota(jnp.int32, (128, 128), 0) == lax.broadcasted_iota(jnp.int32, (128, 128), 1)
    gw = gates_ref[...].astype(f32)
    gw = gw / jnp.sum(gw, axis=0, keepdims=True)
    weight_row = jnp.sum(jnp.where(ids_ref[...] == e, gw, 0.0), axis=0, keepdims=True)
    spot = lax.broadcasted_iota(jnp.int32, (128, 128), 0)
    row = (spot % 64) // 4 * 8 + spot // 64 * 4 + spot % 4
    named = row == lax.broadcasted_iota(jnp.int32, (128, 128), 1)
    weight = jnp.sum(jnp.where(named, weight_row, 0.0), axis=1, keepdims=True)

    def products(slots, first=False):
        for n in range(3):
            for wref, aref in ((wg_v, gate_acc), (wu_v, up_acc)):
                a = None if first else aref[n]
                for src in slots:
                    cols = pl.ds(pl.multiple_of(src * 256, 256), 256)
                    t = nt_dot(hid_all[src].reshape(128, 256), wref[n * 256 : (n + 1) * 256, cols])
                    a = t if a is None else a + t
                aref[n] = a

    for i in range(1, NZ):
        g2.take_z(i)
    loads[3].wait()
    loads[4].wait()
    slots = g2.take_level(0)
    for copy in sq_quad:
        copy.wait_recv()
    sq_total[...] = (sq_level[...] + sq_in[1]) + (sq_in[2] + sq_in[3])

    def sq_z_copy(zz):
        return remote(
            sq_total, sq_z.at[z], q_send.at[4 + zz], q_recv.at[4 + z], (zz * 4 + x * 2 + c, y)
        )

    def sq_z_landing(zz):
        return remote(
            sq_total, sq_z.at[zz], q_send.at[4 + z], q_recv.at[4 + zz], (zz * 4 + x * 2 + c, y)
        )

    for i in range(NZ - 1):
        sq_z_copy(order[i]).start()
    products(slots, True)
    for i in range(1, NZ):
        products(g2.take_level(i) + g2.take_core(i - 1))
    products(g2.take_core(NZ - 1))

    total = sq_total[...]
    for i in range(NZ - 1):
        sq_z_landing(order[i]).wait_recv()
        total = total + sq_z[order[i]]
    scale_row = lax.rsqrt(total[0:1] / 4096.0 + epsilon)
    scale = jnp.sum(jnp.where(eye, scale_row, 0.0), axis=1, keepdims=True)
    for n in range(3):
        g = gate_acc[n] * scale
        u = up_acc[n] * scale
        a = g / (1.0 + jnp.exp(-g)) * u * weight
        a = interleave(a[0:64], a[64:128]).astype(bf16)
        for half in range(2):
            to = pl.ds(pl.multiple_of(((half + y) % 2) * 64, 64), 64)
            act[to, n * 256 : (n + 1) * 256] = a[half * 64 : (half + 1) * 64]
    loads[5].wait()

    def block(zz, xx, cc):
        cols = pl.ds(pl.multiple_of((zz * 4 + xx * 2 + cc) * 256, 256), 256)
        return jnp.dot(act[...], wd_v[:, cols], preferred_element_type=f32)

    def core_copy(zz, k):
        b = k * NZ + zz
        return remote(core_out.at[b], core_in.at[b], r_send.at[b], r_recv.at[b], (ec, y))

    def x_copy(zz):
        return remote(x_out.at[zz], x_in.at[zz], r_send.at[8 + zz], r_recv.at[8 + zz], (ex, y))

    def y_copy(zz):
        return remote(y_out.at[zz], y_in.at[zz], r_send.at[12 + zz], r_recv.at[12 + zz], (e, 1 - y))

    def d_copy(zz):
        return remote(d_out.at[zz], d_in.at[zz], r_send.at[16 + zz], r_recv.at[16 + zz], (ex, 1 - y))

    def z_copy(zz):
        return remote(
            z_out.at[zz], z_in.at[z], r_send.at[20 + zz], r_recv.at[20 + z], (zz * 4 + x * 2 + c, y)
        )

    def z_landing(zz):
        return remote(
            z_out.at[zz], z_in.at[zz], r_send.at[20 + z], r_recv.at[20 + zz], (zz * 4 + x * 2 + c, y)
        )

    def to_core(zz):
        blocks = [block(zz, xx, 1 - c).astype(bf16) for xx in (1 - x, x)]
        for k in range(2):
            core_out[k * NZ + zz] = blocks[k]
            core_copy(zz, k).start()

    def to_plane(zz):
        far, near = block(zz, 1 - x, c), block(zz, x, c)
        core_copy(zz, 0).wait_recv()
        core_copy(zz, 1).wait_recv()
        far = far + core_in[zz].astype(f32)
        near = near + core_in[NZ + zz].astype(f32)
        d_out[zz] = far[64:128].astype(bf16)
        d_copy(zz).start()
        x_out[zz] = far[0:64].astype(bf16)
        x_copy(zz).start()
        y_out[zz] = near[64:128].astype(bf16)
        y_copy(zz).start()
        mine[zz] = near[0:64]

    def plane_sum(zz):
        x_copy(zz).wait_recv()
        y_copy(zz).wait_recv()
        d_copy(zz).wait_recv()
        return mine[zz] + x_in[zz].astype(f32) + (y_in[zz].astype(f32) + d_in[zz].astype(f32))

    to_core(order[0])
    for i in range(NZ):
        if i < NZ - 1:
            to_core(order[i + 1])
        if i == NZ - 1:
            g2.wait_sends()
            rsend.wait_send()
            osend.wait_send()
            osend.wait_recv()
            out_ref[0] = interleave(hid_rows[0].astype(f32), hid_rows[1].astype(f32)).astype(bf16)
            for copy in [sq_core] + sq_quad + [sq_z_copy(order[i]) for i in range(NZ - 1)]:
                copy.wait_send()
        to_plane(order[i])
    for i in range(NZ - 1):
        zz = order[i]
        z_out[zz] = plane_sum(zz).astype(bf16)
        z_copy(zz).start()
        for copy in (core_copy(zz, 0), core_copy(zz, 1), x_copy(zz), y_copy(zz), d_copy(zz)):
            copy.wait_send()
    fin = plane_sum(z)
    for copy in (core_copy(z, 0), core_copy(z, 1), x_copy(z), y_copy(z), d_copy(z)):
        copy.wait_send()
    for i in range(NZ - 1):
        z_copy(order[i]).wait_send()
    for i in range(NZ - 2, -1, -1):
        zz = order[i]
        z_landing(zz).wait_recv()
        fin = fin + z_in[zz].astype(f32)
    out_ref[1] = fin.astype(bf16)


def fused_body(
    query, cache_keys, cache_values, lengths, residual, out_proj, norm_gain, expert_ids, gate_scores,
    w_gate, w_up, w_down,
):
    f32, bf16 = jnp.float32, jnp.bfloat16
    rows = query.shape[0]
    keys = cache_keys.reshape(rows, 512, 128)
    values = cache_values.reshape(rows, 512, 128)
    vm = pl.BlockSpec(memory_space=pltpu.VMEM)
    hb = pl.BlockSpec(memory_space=pl.ANY)
    sm = pl.BlockSpec(memory_space=pltpu.SMEM)
    V, S = pltpu.VMEM, pltpu.SemaphoreType.DMA
    out = pl.pallas_call(
        layer_kernel,
        name="layer",
        out_shape=pltpu.VMEM((2, 64, 256), bf16),
        in_specs=[hb, hb, hb, sm, hb, hb, hb, hb, hb, hb, hb, hb],
        out_specs=vm,
        scratch_shapes=[
            V((rows, 8192), bf16), V((64, 256), bf16), V((256,), bf16), V((8, 128), jnp.int32), V((8, 128), bf16),
            V((rows, 512, 128), bf16), V((rows, 512, 128), bf16), V((256, 4096), bf16),
            V((768, 4096), bf16), V((768, 4096), bf16), V((768, 4096), bf16), S((11,)),
            V((256, 128), f32), V((512, 128), f32), V((2, 16, 1024), bf16), V((16, 2, 16, 1024), bf16),
            V((64, 256), bf16), V((64, 256), bf16),
            V((2, 32, 256), bf16), V((2, 32, 256), bf16), V((2, 32, 256), bf16), V((2, 32, 256), bf16),
            V((16, 2, 64, 256), bf16),
            V((8, 128), f32), V((8, 128), f32), V((8, 128), f32), V((4, 8, 128), f32), V((4, 8, 128), f32),
            V((3, 128, 256), f32), V((3, 128, 256), f32), V((128, 768), bf16),
            V((4, 64, 256), f32), V((8, 128, 256), bf16), V((8, 128, 256), bf16),
            V((4, 64, 256), bf16), V((4, 64, 256), bf16), V((4, 64, 256), bf16), V((4, 64, 256), bf16),
            V((4, 64, 256), bf16), V((4, 64, 256), bf16), V((4, 64, 256), bf16), V((4, 64, 256), bf16),
            S((32,)), S((32,)), S((24,)), S((24,)), S((4,)), S((4,)), S((8,)), S((8,)), S((24,)), S((24,)),
        ],
        compiler_params=pltpu.CompilerParams(
            collective_id=0, has_side_effects=True, vmem_limit_bytes=62 * 1024 * 1024
        ),
    )(
        query, keys, values, lengths, residual, out_proj, norm_gain, expert_ids.T,
        gate_scores.T, w_gate[0], w_up[0], w_down[0],
    )
    return (out[0], out[1])


def solution(mesh):
    in_specs = (
        P(("expert", "tensor"), None),
        P(("expert", "tensor"), None, None, None),
        P(("expert", "tensor"), None, None, None),
        P(("expert", "tensor")),
        P("tensor", "expert"),
        P("expert", "tensor"),
        P("expert"),
        P(),
        P(),
        P("expert", "tensor", None),
        P("expert", "tensor", None),
        P("expert", "tensor", None),
    )
    out_specs = (P("tensor", "expert"), P("tensor", "expert"))
    fused = dict(mesh.shape) == {"expert": 16, "tensor": 2}
    return jax.shard_map(fused_body if fused else body, mesh=mesh, in_specs=in_specs, out_specs=out_specs, check_vma=False)
```
